32 devices in a mesh: section: 4 (over y, x), expert: 8 (over z, core).
Axes of the slice: x: 2, y: 2, z: 4, core: 2. Of those that a mesh axis runs over, the one named last changes fastest.
Arguments:
- sent_fwd: bfloat16 [4, 512, 3584], P('section', 'expert'), may hold values from -6 to 6
- sent_bwd: bfloat16 [4, 512, 3584], P('section', 'expert'), may hold values from -6 to 6
- router_w: float32 [4, 3584, 4], P('section'), may hold values from -0.5 to 0.5
- w_up: bfloat16 [4, 3584, 4096], P('section', None, 'expert'), may hold values from -0.09375 to 0.09375
- w_down: bfloat16 [4, 4096, 3584], P('section', 'expert'), may hold values from -0.1875 to 0.1875
- routes_fwd: int32 [4, 512, 1], P('section', 'expert'), may hold values from 0 to 3; in each aligned block of 64 rows (0 to 63, 64 to 127, ..., all dimensions but the last counted through in order) at most 17 rows name the same one
- routes_bwd: int32 [4, 512, 1], P('section', 'expert'), may hold values from 0 to 3; in each aligned block of 64 rows (0 to 63, 64 to 127, ..., all dimensions but the last counted through in order) at most 17 rows name the same one
Outputs:
- out_fwd: bfloat16 [4, 512, 3584], P('section', 'expert')
- out_bwd: bfloat16 [4, 512, 3584], P('section', 'expert')
The draws below stay inside these ranges and needn't reach their ends.
Inputs may be any that keep to these rules, and one draw needn't show every extreme that they name: `routes_fwd`: at each section the 64 rows of one device name any one expert at most 17 times in all, a bound that some block reaches. `routes_bwd`: at each section the 64 rows of one device name any one expert at most 17 times in all, a bound that some block reaches.
All inputs are finite; a program needn't handle non-finite values.
Results may differ from the reference program's by a relative error of at most 0.003.
Values may be sent and summed in bfloat16 or wider, within the bound.
A program may use at most 128 MiB of HBM per device.

```python
import math
import jax
import jax.numpy as jnp
import numpy as np
from jax import lax

D = 3584
FF = 1024
EXPERTS = 4
TOPK = 1
TOK_DEV = 64
CAP = 17
SPLIT = 2
HID_DEV = 512
HID_ALL = 4096
SECTIONS = 4
TOKENS = 512
N_EXPERT = 8


def levels(rng, shape, pieces, least, top_value):
    gain, own = 1.0, jax.random.fold_in(rng, 6)
    for dim, shards_of in pieces:
        steps = jnp.exp(jax.random.uniform(jax.random.fold_in(own, dim), (shards_of,), jnp.float32, least / len(pieces), top_value / len(pieces)))
        gain = gain * jnp.repeat(steps, shape[dim] // shards_of).reshape([-1 if axis == dim else 1 for axis in range(len(shape))])
    return gain


def deal_out(key, own, number, rows, count, top, bound, slope):
    sequence = jax.random.permutation(key, count)
    heavy_load, ordinary = load_shares(count, rows * top, bound, slope, True), load_shares(count, rows * top, bound, slope, False)
    places = jnp.arange(count)

    def named(tallies, turn):
        used = int((tallies > 0).sum())
        fixed = max(1, used // 4)
        passed = fixed + (places - fixed + turn * (used - fixed)) % max(1, count - fixed)
        return jnp.zeros((count,), jnp.int32).at[sequence[jnp.where(places < fixed, places, passed)]].set(jnp.asarray(tallies, jnp.int32))

    tallies = jnp.where(number % 4 == 0, named(heavy_load, number // 4), named(ordinary, number - number // 4 - 1))
    mixed = jax.random.permutation(jax.random.fold_in(own, 3), count)
    giver, receiver = mixed[0:count // 2 * 2:2], mixed[1:count // 2 * 2:2]
    slack = jnp.minimum(tallies[giver] - 1, bound - tallies[receiver]) // 2
    slack = jnp.where((giver == sequence[0]) | (receiver == sequence[0]) | (tallies[receiver] == 0), 0, jnp.maximum(slack, 0))
    passed = jax.random.randint(jax.random.fold_in(own, 4), (count // 2,), 0, 1 << 20) % (slack + 1)
    tallies = tallies.at[giver].add(-passed).at[receiver].add(passed)
    labels = jnp.searchsorted(jnp.cumsum(tallies), jnp.arange(rows * top), side="right").astype(jnp.int32)
    listing = labels.reshape(top, rows).T
    listing = listing[jax.random.permutation(jax.random.fold_in(own, 1), rows)]
    turn = jax.random.randint(jax.random.fold_in(own, 2), (rows, 1), 0, top)
    return jnp.take_along_axis(listing, (jnp.arange(top)[None, :] + turn) % top, axis=1)


def load_shares(count, total, bound, skew, full):
    loads = [(1 << 20) // math.isqrt(rank ** skew) + 1 for rank in range(1, count + 1)]
    largest = bound if full else min(bound, max(-(-total // count), total * loads[0] // sum(loads)))
    least = 1 if total - largest >= count - 1 else 0
    given, rest = [largest] + [least] * (count - 1), total - largest - least * (count - 1)
    while rest > 0:
        candidates = [i for i in range(1, count) if given[i] < largest] or [i for i in range(1, count) if given[i] < bound]
        whole, remaining = sum([loads[i] for i in candidates]), rest
        for i in candidates:
            extra = min(bound - given[i], max(1, remaining * loads[i] // whole), rest)
            given[i] = given[i] + extra
            rest = rest - extra
    return np.array(given)


def bell_draw(key, dims, width, bound, cuts=(), kind=jnp.bfloat16):
    factor_of = levels(key, dims, cuts, -0.22, 0.18) if cuts else 1.0
    entries = jax.random.normal(key, dims, jnp.float32) * width * factor_of
    return jnp.minimum(jnp.maximum(entries, -bound), bound).astype(kind)


def setup_inputs(seed: int = 0) -> dict:
    streams_of = jax.random.split(jax.random.key(seed), 8)
    sent_fwd = bell_draw(streams_of[0], (SECTIONS, TOKENS, D), 1.0, 6.0, ((0, 4), (1, 8)))
    sent_bwd = bell_draw(streams_of[1], (SECTIONS, TOKENS, D), 1.0, 6.0, ((0, 4), (1, 8)))
    router_w = bell_draw(streams_of[2], (SECTIONS, D, EXPERTS), (2 * D ** -0.5), 0.5, ((0, 4),), jnp.float32)
    w_up = bell_draw(streams_of[3], (SECTIONS, D, HID_ALL), D ** -0.5, 0.09375, ((0, 4), (2, 8)))
    w_down = bell_draw(streams_of[4], (SECTIONS, HID_ALL, D), FF ** -0.5, 0.1875, ((0, 4), (1, 8)))
    routes_fwd_keys = jax.random.split(jax.random.fold_in(streams_of[5], 1), SECTIONS * TOKENS // TOK_DEV)
    routes_fwd_turns = jax.random.permutation(jax.random.fold_in(streams_of[5], 3), SECTIONS * TOKENS // TOK_DEV)
    routes_fwd = jax.vmap(lambda own, number: deal_out(jax.random.fold_in(streams_of[5], 2), own, number, TOK_DEV, EXPERTS, TOPK, CAP, 2))(routes_fwd_keys, routes_fwd_turns).reshape((SECTIONS, TOKENS, TOPK))
    routes_bwd_keys = jax.random.split(jax.random.fold_in(streams_of[6], 1), SECTIONS * TOKENS // TOK_DEV)
    routes_bwd_turns = jax.random.permutation(jax.random.fold_in(streams_of[6], 3), SECTIONS * TOKENS // TOK_DEV)
    routes_bwd = jax.vmap(lambda own, number: deal_out(jax.random.fold_in(streams_of[6], 2), own, number, TOK_DEV, EXPERTS, TOPK, CAP, 2))(routes_bwd_keys, routes_bwd_turns).reshape((SECTIONS, TOKENS, TOPK))
    return {"sent_fwd": sent_fwd, "sent_bwd": sent_bwd, "router_w": router_w, "w_up": w_up, "w_down": w_down, "routes_fwd": routes_fwd, "routes_bwd": routes_bwd}


def moe_layer(inputs, routes, router, up_weights, down_weights):
    chosen = routes.reshape(N_EXPERT, TOK_DEV * TOPK)
    onehot = (chosen[:, :, None] == jnp.arange(EXPERTS, dtype=jnp.int32)[None, None, :]).astype(jnp.int32)
    position = jnp.sum((jnp.cumsum(onehot, axis=1) - 1) * onehot, axis=2)
    source = jnp.arange(N_EXPERT, dtype=jnp.int32)[:, None]
    column = (source * CAP + position).reshape(-1).astype(jnp.int32)
    expert_of = chosen.reshape(-1).astype(jnp.int32)
    rows_in = jnp.repeat(inputs, TOPK, axis=0)
    buffer = jnp.zeros((EXPERTS, N_EXPERT * CAP, D), jnp.bfloat16).at[expert_of, column].set(rows_in)
    up_all = jnp.transpose(up_weights.reshape(D, EXPERTS, FF), (1, 0, 2))
    down_all = down_weights.reshape(EXPERTS, SPLIT, HID_DEV, D)

    def one_expert(operands):
        rows_here, up_expert, down_expert = operands
        hidden = jax.nn.silu(jnp.dot(rows_here, up_expert, preferred_element_type=jnp.float32)).astype(jnp.bfloat16)
        blocks = hidden.reshape(rows_here.shape[0], SPLIT, HID_DEV)
        summed = jnp.zeros((rows_here.shape[0], D), jnp.float32)
        for index_block in range(SPLIT):
            partial_out = jnp.dot(blocks[:, index_block], down_expert[index_block], preferred_element_type=jnp.float32).astype(jnp.bfloat16)
            partial_out = lax.optimization_barrier(partial_out)
            summed = summed + partial_out.astype(jnp.float32)
        return summed

    results = lax.map(one_expert, (buffer, up_all, down_all))
    gathered = results[expert_of, column].reshape(TOKENS, TOPK, D)
    logits = jnp.dot(inputs.astype(jnp.float32), router, precision=lax.Precision.HIGHEST)
    picked = jnp.take_along_axis(logits, routes, axis=1)
    scores = jax.nn.sigmoid(picked)
    mixed = inputs.astype(jnp.float32) + jnp.sum(scores[:, :, None] * gathered, axis=1)
    return mixed.astype(jnp.bfloat16)


def reference(sent_fwd, sent_bwd, router_w, w_up, w_down, routes_fwd, routes_bwd):
    inputs_fwd = jnp.roll(sent_fwd, 1, axis=0)
    inputs_bwd = jnp.roll(sent_bwd, -1, axis=0)

    def one_section(operands):
        first, second, route_first, route_second, router, up_weights, down_weights = operands
        return (moe_layer(first, route_first, router, up_weights, down_weights),
                moe_layer(second, route_second, router, up_weights, down_weights))

    out_fwd, out_bwd = lax.map(one_section, (inputs_fwd, inputs_bwd, routes_fwd, routes_bwd, router_w, w_up, w_down))
    return out_fwd, out_bwd
```

```python
import functools

import jax
import jax.numpy as jnp
from jax import lax
from jax.experimental import pallas as pl
from jax.experimental.pallas import tpu as pltpu
from jax.sharding import PartitionSpec as P

EXPERTS = 4
CAP = 17
PIECES = 2
MESH = pl.DeviceIdType.MESH
F32 = jnp.float32
BF16 = jnp.bfloat16
NT = (((1,), (1,)), ((), ()))


def layer_kernel(
    dims,
    rt_ref, fwd_ref, bwd_ref, router_ref, up_hbm, down_hbm,
    out_fwd, out_bwd,
    x_buf, pack_buf, mine, theirs, acc, hid, part_out, part_in, own_part, y_out, y_in,
    out_buf, up_ref, down_ref, place, place_t, rt_sib, logit_out, logit_in, score_ref,
    relay_s, relay_r, disp_s, disp_r, pair_s, pair_r, part_s, part_r, ret_s, ret_r,
    fin_s, fin_r, loc_s, w_sem, small_s, small_r,
):
    chips, per_expert, sections, tokens, rows, padded, pieces, width = dims
    half = pieces * width
    both = 2 * tokens
    section = lax.axis_index("section")
    me = lax.axis_index("expert")
    core = lax.rem(me, 2)
    chip = me // 2
    sib = {"section": section, "expert": chip * 2 + 1 - core}
    after = lax.rem(section + 1, sections)
    before = lax.rem(section + sections - 1, sections)

    def at_chip(distance):
        return {
            "section": section,
            "expert": lax.rem(chip + distance + chips, chips) * 2 + core,
        }

    def remote(src, dst, send, recv, device):
        return pltpu.make_async_remote_copy(
            src_ref=src, dst_ref=dst, send_sem=send, recv_sem=recv,
            device_id=device, device_id_type=MESH,
        )

    def arrived(dst, send, recv):
        remote(dst, dst, send, recv, sib).wait_recv()

    w_up_copy = pltpu.make_async_copy(up_hbm, up_ref, w_sem.at[0])
    w_down_copy = pltpu.make_async_copy(down_hbm, down_ref, w_sem.at[1])

    tail = padded - 16
    zeros = jnp.zeros((pieces, chips, 16, width), BF16)
    mine[:, :, tail:padded, :] = zeros
    theirs[:, :, tail:padded, :] = zeros
    y_in[:, :, tail:padded, :] = zeros

    barrier = pltpu.get_barrier_semaphore()
    greet = [sib]
    for there in (after, before):
        for j in range(2):
            greet.append({"section": there, "expert": chip * 2 + j})
    for d in range(1, chips):
        greet.append(at_chip(d))
    for device in greet:
        pl.semaphore_signal(barrier, inc=1, device_id=device, device_id_type=MESH)
    pl.semaphore_wait(barrier, len(greet))

    sends = []
    small = remote(rt_ref, rt_sib, small_s.at[0], small_r.at[0], sib)
    small.start()
    sends.append(small)
    for k in range(pieces):
        for m, (source, there) in enumerate(((fwd_ref, after), (bwd_ref, before))):
            for j in range(2):
                copy = remote(
                    source.at[:, pl.ds(j * half + k * width, width)],
                    x_buf.at[k, pl.ds(pl.multiple_of(core * both + m * tokens, tokens), tokens), :],
                    relay_s.at[k, j, m], relay_r.at[k, core, m],
                    {"section": there, "expert": chip * 2 + j},
                )
                copy.start()
                sends.append(copy)
    w_up_copy.start()
    w_down_copy.start()

    small.wait_recv()
    own_routes, sib_routes = rt_ref[...], rt_sib[...]
    first = core == 0
    chosen = jnp.concatenate(
        (jnp.where(first, own_routes, sib_routes), jnp.where(first, sib_routes, own_routes)),
        axis=1,
    )
    count = 2 * both
    named = lax.broadcasted_iota(jnp.int32, (8, count), 0) == chosen
    onehot = jnp.where(named, 1.0, 0.0).astype(F32)
    earlier = lax.broadcasted_iota(jnp.int32, (count, count), 0) <= lax.broadcasted_iota(
        jnp.int32, (count, count), 1
    )
    tri = jnp.where(earlier, 1.0, 0.0).astype(BF16)
    counted = jnp.dot(onehot.astype(BF16), tri, preferred_element_type=F32)
    position = jnp.sum(onehot * (counted - 1.0), axis=0, keepdims=True)
    slots = lax.broadcasted_iota(jnp.int32, (padded, count), 0).astype(F32)
    for d in range(chips):
        expert = lax.rem(chip + d, chips) // per_expert
        here = jnp.where(chosen[0:1, :] == expert, position, -1.0)
        place[d * padded:(d + 1) * padded, :] = jnp.where(slots == here, 1.0, 0.0).astype(BF16)
    eye = lax.broadcasted_iota(jnp.int32, (count, count), 0) == lax.broadcasted_iota(
        jnp.int32, (count, count), 1
    )
    eye = jnp.where(eye, 1.0, 0.0).astype(BF16)
    place_t[...] = lax.dot_general(eye, place[...], NT, preferred_element_type=F32).astype(BF16)

    mine_cols = core * half
    their_cols = (1 - core) * half

    def pair(k, d):
        copy = remote(mine.at[k, d], theirs.at[k, d], pair_s.at[k, d], pair_r.at[k, d], sib)
        copy.start()
        sends.append(copy)

    def stage_pack(k):
        for j in range(2):
            for m in range(2):
                arrived(
                    x_buf.at[k, pl.ds(j * both + m * tokens, tokens), :],
                    relay_s.at[k, j, m], relay_r.at[k, j, m],
                )
        packed = jnp.dot(place[...], x_buf[k], preferred_element_type=F32).astype(BF16)
        packed = packed.reshape(chips, padded, width)
        pack_buf[k] = packed[1:]
        mine[k, 0] = packed[0]
        for d in range(1, chips):
            copy = remote(
                pack_buf.at[k, d - 1, pl.ds(0, rows), :], mine.at[k, d, pl.ds(0, rows), :],
                disp_s.at[k, d], disp_r.at[k, d], at_chip(d),
            )
            copy.start()
            sends.append(copy)
        pair(k, 0)
        cols = pl.ds(pl.multiple_of(mine_cols + k * width, 128), width)
        term = lax.dot_general(
            router_ref[:, cols], x_buf[k].astype(F32), NT,
            precision=lax.Precision.HIGHEST, preferred_element_type=F32,
        )
        logit_out[...] = term if k == 0 else logit_out[...] + term

    def stage_forward(k):
        for d in range(1, chips):
            arrived(mine.at[k, d, pl.ds(0, rows), :], disp_s.at[k, d], disp_r.at[k, d])
            pair(k, d)

    def stage_up(k):
        for d in range(chips):
            arrived(theirs.at[k, d], pair_s.at[k, d], pair_r.at[k, d])
        if k == 0:
            w_up_copy.wait()
        total = jnp.dot(
            mine[k].reshape(chips * padded, width),
            up_ref[pl.ds(pl.multiple_of(mine_cols + k * width, 128), width), :],
            preferred_element_type=F32,
        )
        total += jnp.dot(
            theirs[k].reshape(chips * padded, width),
            up_ref[pl.ds(pl.multiple_of(their_cols + k * width, 128), width), :],
            preferred_element_type=F32,
        )
        acc[...] = total if k == 0 else acc[...] + total

    for step in range(pieces + 2):
        if step < pieces:
            stage_pack(step)
        if step == pieces:
            logits = remote(logit_out, logit_in, small_s.at[1], small_r.at[1], sib)
            logits.start()
            sends.append(logits)
        if 0 <= step - 1 < pieces:
            stage_forward(step - 1)
        if 0 <= step - 2:
            stage_up(step - 2)

    hid[...] = jax.nn.silu(acc[...]).astype(BF16)
    w_down_copy.wait()

    def stage_down(k):
        other = jnp.dot(
            hid[...], down_ref[:, pl.ds(pl.multiple_of(their_cols + k * width, 128), width)],
            preferred_element_type=F32,
        )
        part_out[k] = other.astype(BF16)
        copy = remote(part_out.at[k], part_in.at[k], part_s.at[k], part_r.at[k], sib)
        copy.start()
        sends.append(copy)
        own_part[k] = jnp.dot(
            hid[...], down_ref[:, pl.ds(pl.multiple_of(mine_cols + k * width, 128), width)],
            preferred_element_type=F32,
        ).astype(BF16)

    def stage_return(k):
        arrived(part_in.at[k], part_s.at[k], part_r.at[k])
        y = (own_part[k].astype(F32) + part_in[k].astype(F32)).astype(BF16)
        y = y.reshape(chips, padded, width)
        y_out[k] = y[1:]
        y_in[k, 0, 0:rows, :] = y[0, 0:rows]
        for d in range(1, chips):
            copy = remote(
                y_out.at[k, d - 1, pl.ds(0, rows), :], y_in.at[k, d, pl.ds(0, rows), :],
                ret_s.at[k, d], ret_r.at[k, d], at_chip(-d),
            )
            copy.start()
            sends.append(copy)

    for step in range(pieces + 1):
        if step < pieces:
            stage_down(step)
        if 0 <= step - 1:
            stage_return(step - 1)

    logits.wait_recv()
    picked = jnp.sum(onehot * (logit_out[...] + logit_in[...]), axis=0, keepdims=True)
    score = jax.nn.sigmoid(picked)
    score_ref[...] = jnp.transpose(jnp.broadcast_to(score, (128, count)))

    locals_ = []
    for k in range(pieces):
        for d in range(1, chips):
            arrived(y_in.at[k, d, pl.ds(0, rows), :], ret_s.at[k, d], ret_r.at[k, d])
        gathered = jnp.dot(
            place_t[...], y_in[k].reshape(chips * padded, width), preferred_element_type=F32
        )
        mixed = x_buf[k].astype(F32) + score_ref[:, 0:1] * gathered
        out_buf[k] = mixed.astype(BF16)
        cols = pl.ds(pl.multiple_of(mine_cols + k * width, 128), width)
        for m, out in enumerate((out_fwd, out_bwd)):
            theirs_at = pl.multiple_of((1 - core) * both + m * tokens, tokens)
            copy = remote(
                out_buf.at[k, pl.ds(theirs_at, tokens), :], out.at[:, cols],
                fin_s.at[k, m], fin_r.at[k, m], sib,
            )
            copy.start()
            sends.append(copy)
            mine_at = pl.multiple_of(core * both + m * tokens, tokens)
            local = pltpu.make_async_copy(
                out_buf.at[k, pl.ds(mine_at, tokens), :], out.at[:, cols], loc_s.at[k, m]
            )
            local.start()
            locals_.append(local)

    for local in locals_:
        local.wait()
    for k in range(pieces):
        other_cols = pl.ds(pl.multiple_of(their_cols + k * width, 128), width)
        for m, out in enumerate((out_fwd, out_bwd)):
            arrived(out.at[:, other_cols], fin_s.at[k, m], fin_r.at[k, m])
    for copy in sends:
        copy.wait_send()


def on_device(sent_fwd, sent_bwd, router_w, w_up, w_down, routes_fwd, routes_bwd):
    tokens, model_width = sent_fwd.shape[1:]
    hidden = w_up.shape[2]
    sections = lax.axis_size("section")
    chips = lax.axis_size("expert") // 2
    per_expert = chips // EXPERTS
    rows = -(-4 * CAP // 8) * 8
    padded = -(-4 * CAP // 16) * 16
    pieces = PIECES
    width = model_width // 2 // pieces
    count = 4 * tokens
    dims = (chips, per_expert, sections, tokens, rows, padded, pieces, width)
    routes = jnp.concatenate((routes_fwd.reshape(1, tokens), routes_bwd.reshape(1, tokens)), axis=1)
    routes = jnp.broadcast_to(routes, (8, 2 * tokens))
    router = jnp.pad(router_w[0].T, ((0, 8 - EXPERTS), (0, 0)))
    total = chips * padded
    dma = pltpu.SemaphoreType.DMA
    any_space = pl.BlockSpec(memory_space=pl.ANY)
    vmem = pl.BlockSpec(memory_space=pltpu.VMEM)
    shape = jax.ShapeDtypeStruct((tokens, model_width), BF16)
    out_fwd, out_bwd = pl.pallas_call(
        functools.partial(layer_kernel, dims),
        out_shape=(shape, shape),
        in_specs=[vmem, any_space, any_space, vmem, any_space, any_space],
        out_specs=(any_space, any_space),
        scratch_shapes=[
            pltpu.VMEM((pieces, count, width), BF16),
            pltpu.VMEM((pieces, chips - 1, padded, width), BF16),
            pltpu.VMEM((pieces, chips, padded, width), BF16),
            pltpu.VMEM((pieces, chips, padded, width), BF16),
            pltpu.VMEM((total, hidden), F32),
            pltpu.VMEM((total, hidden), BF16),
            pltpu.VMEM((pieces, total, width), BF16),
            pltpu.VMEM((pieces, total, width), BF16),
            pltpu.VMEM((pieces, total, width), BF16),
            pltpu.VMEM((pieces, chips - 1, padded, width), BF16),
            pltpu.VMEM((pieces, chips, padded, width), BF16),
            pltpu.VMEM((pieces, count, width), BF16),
            pltpu.VMEM((model_width, hidden), BF16),
            pltpu.VMEM((hidden, model_width), BF16),
            pltpu.VMEM((total, count), BF16),
            pltpu.VMEM((count, total), BF16),
            pltpu.VMEM((8, 2 * tokens), jnp.int32),
            pltpu.VMEM((8, count), F32),
            pltpu.VMEM((8, count), F32),
            pltpu.VMEM((count, 128), F32),
            dma((pieces, 2, 2)), dma((pieces, 2, 2)),
            dma((pieces, chips)), dma((pieces, chips)),
            dma((pieces, chips)), dma((pieces, chips)),
            dma((pieces,)), dma((pieces,)),
            dma((pieces, chips)), dma((pieces, chips)),
            dma((pieces, 2)), dma((pieces, 2)),
            dma((pieces, 2)), dma((2,)), dma((2,)), dma((2,)),
        ],
        compiler_params=pltpu.CompilerParams(collective_id=0, has_side_effects=True),
    )(routes, sent_fwd[0], sent_bwd[0], router, w_up[0], w_down[0])
    return out_fwd[None], out_bwd[None]


def solution(mesh):
    return jax.shard_map(
        on_device,
        mesh=mesh,
        in_specs=(
            P("section", "expert", None),
            P("section", "expert", None),
            P("section", None, None),
            P("section", None, "expert"),
            P("section", "expert", None),
            P("section", "expert", None),
            P("section", "expert", None),
        ),
        out_specs=(P("section", "expert", None), P("section", "expert", None)),
        check_vma=False,
    )
```

```python
import functools

import jax
import jax.numpy as jnp
from jax import lax
from jax.experimental import pallas as pl
from jax.experimental.pallas import tpu as pltpu
from jax.sharding import PartitionSpec as P

EXPERTS = 4
CAP = 17
PIECES = 7
MESH = pl.DeviceIdType.MESH
F32 = jnp.float32
BF16 = jnp.bfloat16
NT = (((1,), (1,)), ((), ()))


def layer_kernel(
    dims,
    rt_ref, fwd_ref, bwd_ref, router_ref, up_hbm, down_hbm,
    out_fwd, out_bwd,
    x_buf, pack_buf, mine, theirs, acc, hid, part_out, part_in, own_part, y_out, y_in,
    out_buf, up_ref, down_ref, place, place_t, rt_sib, logit_out, logit_in, score_ref,
    relay_s, relay_r, disp_s, disp_r, pair_s, pair_r, part_s, part_r, ret_s, ret_r,
    fin_s, fin_r, loc_s, w_sem, small_s, small_r,
):
    chips, per_expert, sections, tokens, rows, padded, pieces, width = dims
    half = pieces * width
    both = 2 * tokens
    section = lax.axis_index("section")
    me = lax.axis_index("expert")
    core = lax.rem(me, 2)
    chip = me // 2
    sib = {"section": section, "expert": chip * 2 + 1 - core}
    after = lax.rem(section + 1, sections)
    before = lax.rem(section + sections - 1, sections)

    def at_chip(distance):
        return {
            "section": section,
            "expert": lax.rem(chip + distance + chips, chips) * 2 + core,
        }

    def remote(src, dst, send, recv, device):
        return pltpu.make_async_remote_copy(
            src_ref=src, dst_ref=dst, send_sem=send, recv_sem=recv,
            device_id=device, device_id_type=MESH,
        )

    def arrived(dst, send, recv):
        remote(dst, dst, send, recv, sib).wait_recv()

    w_up_copy = pltpu.make_async_copy(up_hbm, up_ref, w_sem.at[0])
    w_down_copy = pltpu.make_async_copy(down_hbm, down_ref, w_sem.at[1])

    tail = padded - 16
    zeros = jnp.zeros((pieces, chips, 16, width), BF16)
    mine[:, :, tail:padded, :] = zeros
    theirs[:, :, tail:padded, :] = zeros
    y_in[:, :, tail:padded, :] = zeros

    barrier = pltpu.get_barrier_semaphore()
    greet = [sib]
    for there in (after, before):
        for j in range(2):
            greet.append({"section": there, "expert": chip * 2 + j})
    for d in range(1, chips):
        greet.append(at_chip(d))
    for device in greet:
        pl.semaphore_signal(barrier, inc=1, device_id=device, device_id_type=MESH)
    pl.semaphore_wait(barrier, len(greet))

    sends = []
    small = remote(rt_ref, rt_sib, small_s.at[0], small_r.at[0], sib)
    small.start()
    sends.append(small)
    for k in range(pieces):
        for m, (source, there) in enumerate(((fwd_ref, after), (bwd_ref, before))):
            for j in range(2):
                copy = remote(
                    source.at[:, pl.ds(j * half + k * width, width)],
                    x_buf.at[k, pl.ds(pl.multiple_of(core * both + m * tokens, tokens), tokens), :],
                    relay_s.at[k, j, m], relay_r.at[k, core, m],
                    {"section": there, "expert": chip * 2 + j},
                )
                copy.start()
                sends.append(copy)
    w_up_copy.start()
    w_down_copy.start()

    small.wait_recv()
    own_routes, sib_routes = rt_ref[...], rt_sib[...]
    first = core == 0
    chosen = jnp.concatenate(
        (jnp.where(first, own_routes, sib_routes), jnp.where(first, sib_routes, own_routes)),
        axis=1,
    )
    count = 2 * both
    named = lax.broadcasted_iota(jnp.int32, (8, count), 0) == chosen
    onehot = jnp.where(named, 1.0, 0.0).astype(F32)
    earlier = lax.broadcasted_iota(jnp.int32, (count, count), 0) <= lax.broadcasted_iota(
        jnp.int32, (count, count), 1
    )
    tri = jnp.where(earlier, 1.0, 0.0).astype(BF16)
    counted = jnp.dot(onehot.astype(BF16), tri, preferred_element_type=F32)
    position = jnp.sum(onehot * (counted - 1.0), axis=0, keepdims=True)
    slots = lax.broadcasted_iota(jnp.int32, (padded, count), 0).astype(F32)
    for d in range(chips):
        expert = lax.rem(chip + d, chips) // per_expert
        here = jnp.where(chosen[0:1, :] == expert, position, -1.0)
        place[d * padded:(d + 1) * padded, :] = jnp.where(slots == here, 1.0, 0.0).astype(BF16)
    eye = lax.broadcasted_iota(jnp.int32, (count, count), 0) == lax.broadcasted_iota(
        jnp.int32, (count, count), 1
    )
    eye = jnp.where(eye, 1.0, 0.0).astype(BF16)
    place_t[...] = lax.dot_general(eye, place[...], NT, preferred_element_type=F32).astype(BF16)

    mine_cols = core * half
    their_cols = (1 - core) * half

    def pair(k, d):
        copy = remote(mine.at[k, d], theirs.at[k, d], pair_s.at[k, d], pair_r.at[k, d], sib)
        copy.start()
        sends.append(copy)

    def stage_pack(k):
        for j in range(2):
            for m in range(2):
                arrived(
                    x_buf.at[k, pl.ds(j * both + m * tokens, tokens), :],
                    relay_s.at[k, j, m], relay_r.at[k, j, m],
                )
        packed = jnp.dot(place[...], x_buf[k], preferred_element_type=F32).astype(BF16)
        packed = packed.reshape(chips, padded, width)
        pack_buf[k] = packed[1:]
        mine[k, 0] = packed[0]
        for d in range(1, chips):
            copy = remote(
                pack_buf.at[k, d - 1, pl.ds(0, rows), :], mine.at[k, d, pl.ds(0, rows), :],
                disp_s.at[k, d], disp_r.at[k, d], at_chip(d),
            )
            copy.start()
            sends.append(copy)
        pair(k, 0)
        cols = pl.ds(pl.multiple_of(mine_cols + k * width, 128), width)
        term = lax.dot_general(
            router_ref[:, cols], x_buf[k].astype(F32), NT,
            precision=lax.Precision.HIGHEST, preferred_element_type=F32,
        )
        logit_out[...] = term if k == 0 else logit_out[...] + term

    def stage_forward(k):
        for d in range(1, chips):
            arrived(mine.at[k, d, pl.ds(0, rows), :], disp_s.at[k, d], disp_r.at[k, d])
            pair(k, d)

    def stage_up(k):
        for d in range(chips):
            arrived(theirs.at[k, d], pair_s.at[k, d], pair_r.at[k, d])
        if k == 0:
            w_up_copy.wait()
        total = jnp.dot(
            mine[k].reshape(chips * padded, width),
            up_ref[pl.ds(pl.multiple_of(mine_cols + k * width, 128), width), :],
            preferred_element_type=F32,
        )
        total += jnp.dot(
            theirs[k].reshape(chips * padded, width),
            up_ref[pl.ds(pl.multiple_of(their_cols + k * width, 128), width), :],
            preferred_element_type=F32,
        )
        acc[...] = total if k == 0 else acc[...] + total

    for step in range(pieces + 2):
        if step < pieces:
            stage_pack(step)
        if step == pieces:
            logits = remote(logit_out, logit_in, small_s.at[1], small_r.at[1], sib)
            logits.start()
            sends.append(logits)
        if 0 <= step - 1 < pieces:
            stage_forward(step - 1)
        if 0 <= step - 2:
            stage_up(step - 2)

    hid[...] = jax.nn.silu(acc[...]).astype(BF16)
    w_down_copy.wait()

    def stage_down(k):
        other = jnp.dot(
            hid[...], down_ref[:, pl.ds(pl.multiple_of(their_cols + k * width, 128), width)],
            preferred_element_type=F32,
        )
        part_out[k] = other.astype(BF16)
        copy = remote(part_out.at[k], part_in.at[k], part_s.at[k], part_r.at[k], sib)
        copy.start()
        sends.append(copy)
        own_part[k] = jnp.dot(
            hid[...], down_ref[:, pl.ds(pl.multiple_of(mine_cols + k * width, 128), width)],
            preferred_element_type=F32,
        ).astype(BF16)

    def stage_return(k):
        arrived(part_in.at[k], part_s.at[k], part_r.at[k])
        y = (own_part[k].astype(F32) + part_in[k].astype(F32)).astype(BF16)
        y = y.reshape(chips, padded, width)
        y_out[k] = y[1:]
        y_in[k, 0, 0:rows, :] = y[0, 0:rows]
        for d in range(1, chips):
            copy = remote(
                y_out.at[k, d - 1, pl.ds(0, rows), :], y_in.at[k, d, pl.ds(0, rows), :],
                ret_s.at[k, d], ret_r.at[k, d], at_chip(-d),
            )
            copy.start()
            sends.append(copy)

    for step in range(pieces + 1):
        if step < pieces:
            stage_down(step)
        if 0 <= step - 1:
            stage_return(step - 1)

    logits.wait_recv()
    picked = jnp.sum(onehot * (logit_out[...] + logit_in[...]), axis=0, keepdims=True)
    score = jax.nn.sigmoid(picked)
    score_ref[...] = jnp.transpose(jnp.broadcast_to(score, (128, count)))

    locals_ = []
    for k in range(pieces):
        for d in range(1, chips):
            arrived(y_in.at[k, d, pl.ds(0, rows), :], ret_s.at[k, d], ret_r.at[k, d])
        gathered = jnp.dot(
            place_t[...], y_in[k].reshape(chips * padded, width), preferred_element_type=F32
        )
        mixed = x_buf[k].astype(F32) + score_ref[:, 0:1] * gathered
        out_buf[k] = mixed.astype(BF16)
        cols = pl.ds(pl.multiple_of(mine_cols + k * width, 128), width)
        for m, out in enumerate((out_fwd, out_bwd)):
            theirs_at = pl.multiple_of((1 - core) * both + m * tokens, tokens)
            copy = remote(
                out_buf.at[k, pl.ds(theirs_at, tokens), :], out.at[:, cols],
                fin_s.at[k, m], fin_r.at[k, m], sib,
            )
            copy.start()
            sends.append(copy)
            mine_at = pl.multiple_of(core * both + m * tokens, tokens)
            local = pltpu.make_async_copy(
                out_buf.at[k, pl.ds(mine_at, tokens), :], out.at[:, cols], loc_s.at[k, m]
            )
            local.start()
            locals_.append(local)

    for local in locals_:
        local.wait()
    for k in range(pieces):
        other_cols = pl.ds(pl.multiple_of(their_cols + k * width, 128), width)
        for m, out in enumerate((out_fwd, out_bwd)):
            arrived(out.at[:, other_cols], fin_s.at[k, m], fin_r.at[k, m])
    for copy in sends:
        copy.wait_send()


def on_device(sent_fwd, sent_bwd, router_w, w_up, w_down, routes_fwd, routes_bwd):
    tokens, model_width = sent_fwd.shape[1:]
    hidden = w_up.shape[2]
    sections = lax.axis_size("section")
    chips = lax.axis_size("expert") // 2
    per_expert = chips // EXPERTS
    rows = -(-4 * CAP // 8) * 8
    padded = -(-4 * CAP // 16) * 16
    pieces = PIECES
    width = model_width // 2 // pieces
    count = 4 * tokens
    dims = (chips, per_expert, sections, tokens, rows, padded, pieces, width)
    routes = jnp.concatenate((routes_fwd.reshape(1, tokens), routes_bwd.reshape(1, tokens)), axis=1)
    routes = jnp.broadcast_to(routes, (8, 2 * tokens))
    router = jnp.pad(router_w[0].T, ((0, 8 - EXPERTS), (0, 0)))
    total = chips * padded
    dma = pltpu.SemaphoreType.DMA
    any_space = pl.BlockSpec(memory_space=pl.ANY)
    vmem = pl.BlockSpec(memory_space=pltpu.VMEM)
    shape = jax.ShapeDtypeStruct((tokens, model_width), BF16)
    out_fwd, out_bwd = pl.pallas_call(
        functools.partial(layer_kernel, dims),
        out_shape=(shape, shape),
        in_specs=[vmem, any_space, any_space, vmem, any_space, any_space],
        out_specs=(any_space, any_space),
        scratch_shapes=[
            pltpu.VMEM((pieces, count, width), BF16),
            pltpu.VMEM((pieces, chips - 1, padded, width), BF16),
            pltpu.VMEM((pieces, chips, padded, width), BF16),
            pltpu.VMEM((pieces, chips, padded, width), BF16),
            pltpu.VMEM((total, hidden), F32),
            pltpu.VMEM((total, hidden), BF16),
            pltpu.VMEM((pieces, total, width), BF16),
            pltpu.VMEM((pieces, total, width), BF16),
            pltpu.VMEM((pieces, total, width), BF16),
            pltpu.VMEM((pieces, chips - 1, padded, width), BF16),
            pltpu.VMEM((pieces, chips, padded, width), BF16),
            pltpu.VMEM((pieces, count, width), BF16),
            pltpu.VMEM((model_width, hidden), BF16),
            pltpu.VMEM((hidden, model_width), BF16),
            pltpu.VMEM((total, count), BF16),
            pltpu.VMEM((count, total), BF16),
            pltpu.VMEM((8, 2 * tokens), jnp.int32),
            pltpu.VMEM((8, count), F32),
            pltpu.VMEM((8, count), F32),
            pltpu.VMEM((count, 128), F32),
            dma((pieces, 2, 2)), dma((pieces, 2, 2)),
            dma((pieces, chips)), dma((pieces, chips)),
            dma((pieces, chips)), dma((pieces, chips)),
            dma((pieces,)), dma((pieces,)),
            dma((pieces, chips)), dma((pieces, chips)),
            dma((pieces, 2)), dma((pieces, 2)),
            dma((pieces, 2)), dma((2,)), dma((2,)), dma((2,)),
        ],
        compiler_params=pltpu.CompilerParams(collective_id=0, has_side_effects=True),
    )(routes, sent_fwd[0], sent_bwd[0], router, w_up[0], w_down[0])
    return out_fwd[None], out_bwd[None]


def solution(mesh):
    return jax.shard_map(
        on_device,
        mesh=mesh,
        in_specs=(
            P("section", "expert", None),
            P("section", "expert", None),
            P("section", None, None),
            P("section", None, "expert"),
            P("section", "expert", None),
            P("section", "expert", None),
            P("section", "expert", None),
        ),
        out_specs=(P("section", "expert", None), P("section", "expert", None)),
        check_vma=False,
    )
```

```python
import functools

import jax
import jax.numpy as jnp
from jax import lax
from jax.experimental import pallas as pl
from jax.experimental.pallas import tpu as pltpu
from jax.sharding import PartitionSpec as P

EXPERTS = 4
CAP = 17
PIECES = 7
MESH = pl.DeviceIdType.MESH
F32 = jnp.float32
BF16 = jnp.bfloat16
NT = (((1,), (1,)), ((), ()))


def layer_kernel(
    dims,
    rf_ref, rb_ref, fwd_ref, bwd_ref, router_ref, up_hbm, down_hbm,
    out_fwd, out_bwd,
    x_buf, pack_buf, mine, theirs, acc, hid, part_out, part_in, own_part, y_out, y_in,
    out_buf, up_ref, down_ref, place, place_t, rt_sib, logit_out, logit_in, score_ref,
    relay_s, relay_r, disp_s, disp_r, pair_s, pair_r, part_s, part_r, ret_s, ret_r,
    fin_s, fin_r, loc_s, w_sem, small_s, small_r,
):
    chips, per_expert, sections, tokens, rows, padded, pieces, width = dims
    half = pieces * width
    both = 2 * tokens
    section = lax.axis_index("section")
    me = lax.axis_index("expert")
    core = lax.rem(me, 2)
    chip = me // 2
    sib = {"section": section, "expert": chip * 2 + 1 - core}
    after = lax.rem(section + 1, sections)
    before = lax.rem(section + sections - 1, sections)

    def partner(v):
        other, bit = chip, 1
        while bit <= v:
            if (v // bit) % 2:
                other = other + bit - 2 * bit * lax.rem(chip // bit, 2)
            bit *= 2
        return other

    def at_chip(v):
        return {"section": section, "expert": partner(v) * 2 + core}

    order = [v for v in range(chips // 2, chips)] + [v for v in range(1, chips // 2)]

    def remote(src, dst, send, recv, device):
        return pltpu.make_async_remote_copy(
            src_ref=src, dst_ref=dst, send_sem=send, recv_sem=recv,
            device_id=device, device_id_type=MESH,
        )

    def arrived(dst, send, recv):
        remote(dst, dst, send, recv, sib).wait_recv()

    w_up_copy = pltpu.make_async_copy(up_hbm, up_ref, w_sem.at[0])
    w_down_copy = pltpu.make_async_copy(down_hbm, down_ref, w_sem.at[1])

    tail = padded - 16
    zeros = jnp.zeros((pieces, chips, 16, width), BF16)
    mine[:, :, tail:padded, :] = zeros
    theirs[:, :, tail:padded, :] = zeros
    y_in[:, :, tail:padded, :] = zeros

    barrier = pltpu.get_barrier_semaphore()
    greet = [sib]
    for there in (after, before):
        for j in range(2):
            greet.append({"section": there, "expert": chip * 2 + j})
    for d in order:
        greet.append(at_chip(d))
    for device in greet:
        pl.semaphore_signal(barrier, inc=1, device_id=device, device_id_type=MESH)
    pl.semaphore_wait(barrier, len(greet))

    sends = []
    route_copies = []
    for m, ref in enumerate((rf_ref, rb_ref)):
        copy = remote(ref, rt_sib.at[m], small_s.at[m], small_r.at[m], sib)
        copy.start()
        sends.append(copy)
        route_copies.append(copy)
    for k in range(pieces):
        for m, (source, there) in enumerate(((fwd_ref, after), (bwd_ref, before))):
            for j in range(2):
                copy = remote(
                    source.at[:, pl.ds(j * half + k * width, width)],
                    x_buf.at[k, pl.ds(pl.multiple_of(core * both + m * tokens, tokens), tokens), :],
                    relay_s.at[k, j, m], relay_r.at[k, core, m],
                    {"section": there, "expert": chip * 2 + j},
                )
                copy.start()
                sends.append(copy)
    w_up_copy.start()
    w_down_copy.start()

    for copy in route_copies:
        copy.wait_recv()
    own = (rf_ref[...], rb_ref[...])
    sibs = (rt_sib[0], rt_sib[1])
    first = core == 0
    chosen = jnp.concatenate(
        [jnp.where(first, a, b) for a, b in zip(own, sibs)]
        + [jnp.where(first, b, a) for a, b in zip(own, sibs)],
        axis=1,
    )
    count = 2 * both
    named = lax.broadcasted_iota(jnp.int32, (EXPERTS, count), 0) == chosen
    onehot = jnp.where(named, 1.0, 0.0).astype(F32)
    earlier = lax.broadcasted_iota(jnp.int32, (count, count), 0) <= lax.broadcasted_iota(
        jnp.int32, (count, count), 1
    )
    tri = jnp.where(earlier, 1.0, 0.0).astype(BF16)
    counted = jnp.dot(onehot.astype(BF16), tri, preferred_element_type=F32)
    position = jnp.sum(onehot * (counted - 1.0), axis=0, keepdims=True)
    slots = lax.broadcasted_iota(jnp.int32, (padded, count), 0).astype(F32)
    for d in range(chips):
        expert = partner(d) // per_expert
        here = jnp.where(chosen == expert, position, -1.0)
        place[d * padded:(d + 1) * padded, :] = jnp.where(slots == here, 1.0, 0.0).astype(BF16)
    eye = lax.broadcasted_iota(jnp.int32, (count, count), 0) == lax.broadcasted_iota(
        jnp.int32, (count, count), 1
    )
    eye = jnp.where(eye, 1.0, 0.0).astype(BF16)
    place_t[...] = lax.dot_general(eye, place[...], NT, preferred_element_type=F32).astype(BF16)

    mine_cols = core * half
    their_cols = (1 - core) * half

    def pair(k, d):
        copy = remote(mine.at[k, d], theirs.at[k, d], pair_s.at[k, d], pair_r.at[k, d], sib)
        copy.start()
        sends.append(copy)

    def stage_pack(k):
        for j in range(2):
            for m in range(2):
                arrived(
                    x_buf.at[k, pl.ds(j * both + m * tokens, tokens), :],
                    relay_s.at[k, j, m], relay_r.at[k, j, m],
                )
        packed = jnp.dot(place[...], x_buf[k], preferred_element_type=F32).astype(BF16)
        packed = packed.reshape(chips, padded, width)
        pack_buf[k] = packed[1:]
        mine[k, 0] = packed[0]
        for d in order:
            copy = remote(
                pack_buf.at[k, d - 1, pl.ds(0, rows), :], mine.at[k, d, pl.ds(0, rows), :],
                disp_s.at[k, d], disp_r.at[k, d], at_chip(d),
            )
            copy.start()
            sends.append(copy)
        pair(k, 0)
        cols = pl.ds(pl.multiple_of(mine_cols + k * width, 128), width)
        term = lax.dot_general(
            router_ref[:, cols], x_buf[k].astype(F32), NT,
            precision=lax.Precision.HIGHEST, preferred_element_type=F32,
        )
        logit_out[...] = term if k == 0 else logit_out[...] + term

    def stage_forward(k):
        for d in order:
            arrived(mine.at[k, d, pl.ds(0, rows), :], disp_s.at[k, d], disp_r.at[k, d])
            pair(k, d)

    def stage_up(k):
        for d in range(chips):
            arrived(theirs.at[k, d], pair_s.at[k, d], pair_r.at[k, d])
        if k == 0:
            w_up_copy.wait()
        total = jnp.dot(
            mine[k].reshape(chips * padded, width),
            up_ref[pl.ds(pl.multiple_of(mine_cols + k * width, 128), width), :],
            preferred_element_type=F32,
        )
        total += jnp.dot(
            theirs[k].reshape(chips * padded, width),
            up_ref[pl.ds(pl.multiple_of(their_cols + k * width, 128), width), :],
            preferred_element_type=F32,
        )
        acc[...] = total if k == 0 else acc[...] + total

    for step in range(pieces + 2):
        if step < pieces:
            stage_pack(step)
        if step == pieces:
            logits = remote(logit_out, logit_in, small_s.at[2], small_r.at[2], sib)
            logits.start()
            sends.append(logits)
        if 0 <= step - 1 < pieces:
            stage_forward(step - 1)
        if 0 <= step - 2:
            stage_up(step - 2)

    hid[...] = jax.nn.silu(acc[...]).astype(BF16)
    w_down_copy.wait()

    def stage_down(k):
        other = jnp.dot(
            hid[...], down_ref[:, pl.ds(pl.multiple_of(their_cols + k * width, 128), width)],
            preferred_element_type=F32,
        )
        part_out[k] = other.astype(BF16)
        copy = remote(part_out.at[k], part_in.at[k], part_s.at[k], part_r.at[k], sib)
        copy.start()
        sends.append(copy)
        own_part[k] = jnp.dot(
            hid[...], down_ref[:, pl.ds(pl.multiple_of(mine_cols + k * width, 128), width)],
            preferred_element_type=F32,
        ).astype(BF16)

    def stage_return(k):
        arrived(part_in.at[k], part_s.at[k], part_r.at[k])
        y = (own_part[k].astype(F32) + part_in[k].astype(F32)).astype(BF16)
        y = y.reshape(chips, padded, width)
        y_out[k] = y[1:]
        y_in[k, 0, 0:rows, :] = y[0, 0:rows]
        for d in order:
            copy = remote(
                y_out.at[k, d - 1, pl.ds(0, rows), :], y_in.at[k, d, pl.ds(0, rows), :],
                ret_s.at[k, d], ret_r.at[k, d], at_chip(d),
            )
            copy.start()
            sends.append(copy)

    for step in range(pieces + 1):
        if step < pieces:
            stage_down(step)
        if 0 <= step - 1:
            stage_return(step - 1)

    logits.wait_recv()
    picked = jnp.sum(onehot * (logit_out[...] + logit_in[...]), axis=0, keepdims=True)
    score = jax.nn.sigmoid(picked)
    score_ref[...] = jnp.transpose(jnp.broadcast_to(score, (128, count)))

    locals_ = []
    for k in range(pieces):
        for d in range(1, chips):
            arrived(y_in.at[k, d, pl.ds(0, rows), :], ret_s.at[k, d], ret_r.at[k, d])
        gathered = jnp.dot(
            place_t[...], y_in[k].reshape(chips * padded, width), preferred_element_type=F32
        )
        mixed = x_buf[k].astype(F32) + score_ref[:, 0:1] * gathered
        out_buf[k] = mixed.astype(BF16)
        cols = pl.ds(pl.multiple_of(mine_cols + k * width, 128), width)
        for m, out in enumerate((out_fwd, out_bwd)):
            theirs_at = pl.multiple_of((1 - core) * both + m * tokens, tokens)
            copy = remote(
                out_buf.at[k, pl.ds(theirs_at, tokens), :], out.at[:, cols],
                fin_s.at[k, m], fin_r.at[k, m], sib,
            )
            copy.start()
            sends.append(copy)
            mine_at = pl.multiple_of(core * both + m * tokens, tokens)
            local = pltpu.make_async_copy(
                out_buf.at[k, pl.ds(mine_at, tokens), :], out.at[:, cols], loc_s.at[k, m]
            )
            local.start()
            locals_.append(local)

    for local in locals_:
        local.wait()
    for k in range(pieces):
        other_cols = pl.ds(pl.multiple_of(their_cols + k * width, 128), width)
        for m, out in enumerate((out_fwd, out_bwd)):
            arrived(out.at[:, other_cols], fin_s.at[k, m], fin_r.at[k, m])
    for copy in sends:
        copy.wait_send()


def write_kernel(a_ref, b_ref, out_a, out_b, held, in_sem, out_sem):
    pairs = ((a_ref, out_a), (b_ref, out_b))
    loads = [pltpu.make_async_copy(src, held.at[i], in_sem.at[i]) for i, (src, _) in enumerate(pairs)]
    stores = [pltpu.make_async_copy(held.at[i], dst, out_sem.at[i]) for i, (_, dst) in enumerate(pairs)]
    for load in loads:
        load.start()
    for load, store in zip(loads, stores):
        load.wait()
        store.start()
    for store in stores:
        store.wait()


def on_device(sent_fwd, sent_bwd, router_w, w_up, w_down, routes_fwd, routes_bwd):
    tokens, model_width = sent_fwd.shape[1:]
    hidden = w_up.shape[2]
    sections = lax.axis_size("section")
    chips = lax.axis_size("expert") // 2
    per_expert = chips // EXPERTS
    rows = -(-4 * CAP // 8) * 8
    padded = -(-4 * CAP // 16) * 16
    pieces = PIECES
    width = model_width // 2 // pieces
    count = 4 * tokens
    dims = (chips, per_expert, sections, tokens, rows, padded, pieces, width)
    router = router_w[0].T
    total = chips * padded
    dma = pltpu.SemaphoreType.DMA
    any_space = pl.BlockSpec(memory_space=pl.ANY)
    vmem = pl.BlockSpec(memory_space=pltpu.VMEM)
    shape = jax.ShapeDtypeStruct((tokens, model_width), BF16)
    out_fwd, out_bwd = pl.pallas_call(
        functools.partial(layer_kernel, dims),
        out_shape=(shape, shape),
        in_specs=[vmem, vmem, any_space, any_space, vmem, any_space, any_space],
        out_specs=(any_space, any_space),
        scratch_shapes=[
            pltpu.VMEM((pieces, count, width), BF16),
            pltpu.VMEM((pieces, chips - 1, padded, width), BF16),
            pltpu.VMEM((pieces, chips, padded, width), BF16),
            pltpu.VMEM((pieces, chips, padded, width), BF16),
            pltpu.VMEM((total, hidden), F32),
            pltpu.VMEM((total, hidden), BF16),
            pltpu.VMEM((pieces, total, width), BF16),
            pltpu.VMEM((pieces, total, width), BF16),
            pltpu.VMEM((pieces, total, width), BF16),
            pltpu.VMEM((pieces, chips - 1, padded, width), BF16),
            pltpu.VMEM((pieces, chips, padded, width), BF16),
            pltpu.VMEM((pieces, count, width), BF16),
            pltpu.VMEM((model_width, hidden), BF16),
            pltpu.VMEM((hidden, model_width), BF16),
            pltpu.VMEM((total, count), BF16),
            pltpu.VMEM((count, total), BF16),
            pltpu.VMEM((2, 1, tokens), jnp.int32),
            pltpu.VMEM((EXPERTS, count), F32),
            pltpu.VMEM((EXPERTS, count), F32),
            pltpu.VMEM((count, 128), F32),
            dma((pieces, 2, 2)), dma((pieces, 2, 2)),
            dma((pieces, chips)), dma((pieces, chips)),
            dma((pieces, chips)), dma((pieces, chips)),
            dma((pieces,)), dma((pieces,)),
            dma((pieces, chips)), dma((pieces, chips)),
            dma((pieces, 2)), dma((pieces, 2)),
            dma((pieces, 2)), dma((2,)), dma((3,)), dma((3,)),
        ],
        compiler_params=pltpu.CompilerParams(collective_id=0, has_side_effects=True),
    )(
        routes_fwd.reshape(1, tokens), routes_bwd.reshape(1, tokens),
        sent_fwd[0], sent_bwd[0], router, w_up[0], w_down[0],
    )
    out_fwd, out_bwd = pl.pallas_call(
        write_kernel,
        out_shape=(shape, shape),
        in_specs=[any_space, any_space],
        out_specs=(any_space, any_space),
        scratch_shapes=[pltpu.VMEM((2, tokens, model_width), BF16), dma((2,)), dma((2,))],
        compiler_params=pltpu.CompilerParams(has_side_effects=True),
    )(out_fwd, out_bwd)
    return out_fwd[None], out_bwd[None]


def solution(mesh):
    return jax.shard_map(
        on_device,
        mesh=mesh,
        in_specs=(
            P("section", "expert", None),
            P("section", "expert", None),
            P("section", None, None),
            P("section", None, "expert"),
            P("section", "expert", None),
            P("section", "expert", None),
            P("section", "expert", None),
        ),
        out_specs=(P("section", "expert", None), P("section", "expert", None)),
        check_vma=False,
    )
```

```python
import functools

import jax
import jax.numpy as jnp
from jax import lax
from jax.experimental import pallas as pl
from jax.experimental.pallas import tpu as pltpu
from jax.sharding import PartitionSpec as P

EXPERTS = 4
CAP = 17
PIECES = 14
MESH = pl.DeviceIdType.MESH
F32 = jnp.float32
BF16 = jnp.bfloat16
NT = (((1,), (1,)), ((), ()))


def layer_kernel(
    dims,
    rf_ref, rb_ref, fwd_ref, bwd_ref, router_ref, up_hbm, down_hbm,
    out_fwd, out_bwd,
    x_buf, pack_buf, mine, theirs, acc, hid, part_out, part_in, own_part, y_out, y_in,
    out_buf, up_ref, down_ref, place, place_t, rt_sib, logit_out, logit_in, score_ref,
    relay_s, relay_r, disp_s, disp_r, pair_s, pair_r, part_s, part_r, ret_s, ret_r,
    fin_s, fin_r, loc_s, w_sem, small_s, small_r,
):
    chips, per_expert, sections, tokens, rows, padded, pieces, width = dims
    half = pieces * width
    both = 2 * tokens
    section = lax.axis_index("section")
    me = lax.axis_index("expert")
    core = lax.rem(me, 2)
    chip = me // 2
    sib = {"section": section, "expert": chip * 2 + 1 - core}
    after = lax.rem(section + 1, sections)
    before = lax.rem(section + sections - 1, sections)

    def partner(v):
        other, bit = chip, 1
        while bit <= v:
            if (v // bit) % 2:
                other = other + bit - 2 * bit * lax.rem(chip // bit, 2)
            bit *= 2
        return other

    def at_chip(v):
        return {"section": section, "expert": partner(v) * 2 + core}

    order = [v for v in range(chips // 2, chips)] + [v for v in range(1, chips // 2)]

    def remote(src, dst, send, recv, device):
        return pltpu.make_async_remote_copy(
            src_ref=src, dst_ref=dst, send_sem=send, recv_sem=recv,
            device_id=device, device_id_type=MESH,
        )

    def arrived(dst, send, recv):
        remote(dst, dst, send, recv, sib).wait_recv()

    w_up_copy = pltpu.make_async_copy(up_hbm, up_ref, w_sem.at[0])
    w_down_copy = pltpu.make_async_copy(down_hbm, down_ref, w_sem.at[1])

    tail = padded - 16
    zeros = jnp.zeros((pieces, chips, 16, width), BF16)
    mine[:, :, tail:padded, :] = zeros
    theirs[:, :, tail:padded, :] = zeros
    y_in[:, :, tail:padded, :] = zeros

    barrier = pltpu.get_barrier_semaphore()
    greet = [sib]
    for there in (after, before):
        for j in range(2):
            greet.append({"section": there, "expert": chip * 2 + j})
    for d in order:
        greet.append(at_chip(d))
    for device in greet:
        pl.semaphore_signal(barrier, inc=1, device_id=device, device_id_type=MESH)
    pl.semaphore_wait(barrier, len(greet))

    sends = []
    route_copies = []
    for m, ref in enumerate((rf_ref, rb_ref)):
        copy = remote(ref, rt_sib.at[m], small_s.at[m], small_r.at[m], sib)
        copy.start()
        sends.append(copy)
        route_copies.append(copy)
    for k in range(pieces):
        for m, (source, there) in enumerate(((fwd_ref, after), (bwd_ref, before))):
            for j in range(2):
                copy = remote(
                    source.at[:, pl.ds(j * half + k * width, width)],
                    x_buf.at[k, pl.ds(pl.multiple_of(core * both + m * tokens, tokens), tokens), :],
                    relay_s.at[k, j, m], relay_r.at[k, core, m],
                    {"section": there, "expert": chip * 2 + j},
                )
                copy.start()
                sends.append(copy)
    w_up_copy.start()
    w_down_copy.start()

    for copy in route_copies:
        copy.wait_recv()
    own = (rf_ref[...], rb_ref[...])
    sibs = (rt_sib[0], rt_sib[1])
    first = core == 0
    chosen = jnp.concatenate(
        [jnp.where(first, a, b) for a, b in zip(own, sibs)]
        + [jnp.where(first, b, a) for a, b in zip(own, sibs)],
        axis=1,
    )
    count = 2 * both
    named = lax.broadcasted_iota(jnp.int32, (EXPERTS, count), 0) == chosen
    onehot = jnp.where(named, 1.0, 0.0).astype(F32)
    earlier = lax.broadcasted_iota(jnp.int32, (count, count), 0) <= lax.broadcasted_iota(
        jnp.int32, (count, count), 1
    )
    tri = jnp.where(earlier, 1.0, 0.0).astype(BF16)
    counted = jnp.dot(onehot.astype(BF16), tri, preferred_element_type=F32)
    position = jnp.sum(onehot * (counted - 1.0), axis=0, keepdims=True)
    slots = lax.broadcasted_iota(jnp.int32, (padded, count), 0).astype(F32)
    for d in range(chips):
        expert = partner(d) // per_expert
        here = jnp.where(chosen == expert, position, -1.0)
        place[d * padded:(d + 1) * padded, :] = jnp.where(slots == here, 1.0, 0.0).astype(BF16)
    eye = lax.broadcasted_iota(jnp.int32, (count, count), 0) == lax.broadcasted_iota(
        jnp.int32, (count, count), 1
    )
    eye = jnp.where(eye, 1.0, 0.0).astype(BF16)
    place_t[...] = lax.dot_general(eye, place[...], NT, preferred_element_type=F32).astype(BF16)

    mine_cols = core * half
    their_cols = (1 - core) * half

    def pair(k, d):
        copy = remote(mine.at[k, d], theirs.at[k, d], pair_s.at[k, d], pair_r.at[k, d], sib)
        copy.start()
        sends.append(copy)

    def stage_pack(k):
        for j in range(2):
            for m in range(2):
                arrived(
                    x_buf.at[k, pl.ds(j * both + m * tokens, tokens), :],
                    relay_s.at[k, j, m], relay_r.at[k, j, m],
                )
        packed = jnp.dot(place[...], x_buf[k], preferred_element_type=F32).astype(BF16)
        packed = packed.reshape(chips, padded, width)
        pack_buf[k] = packed[1:]
        mine[k, 0] = packed[0]
        for d in order:
            copy = remote(
                pack_buf.at[k, d - 1, pl.ds(0, rows), :], mine.at[k, d, pl.ds(0, rows), :],
                disp_s.at[k, d], disp_r.at[k, d], at_chip(d),
            )
            copy.start()
            sends.append(copy)
        pair(k, 0)
        cols = pl.ds(pl.multiple_of(mine_cols + k * width, 128), width)
        term = lax.dot_general(
            router_ref[:, cols], x_buf[k].astype(F32), NT,
            precision=lax.Precision.HIGHEST, preferred_element_type=F32,
        )
        logit_out[...] = term if k == 0 else logit_out[...] + term

    def stage_forward(k):
        for d in order:
            arrived(mine.at[k, d, pl.ds(0, rows), :], disp_s.at[k, d], disp_r.at[k, d])
            pair(k, d)

    def stage_up(k):
        for d in range(chips):
            arrived(theirs.at[k, d], pair_s.at[k, d], pair_r.at[k, d])
        if k == 0:
            w_up_copy.wait()
        total = jnp.dot(
            mine[k].reshape(chips * padded, width),
            up_ref[pl.ds(pl.multiple_of(mine_cols + k * width, 128), width), :],
            preferred_element_type=F32,
        )
        total += jnp.dot(
            theirs[k].reshape(chips * padded, width),
            up_ref[pl.ds(pl.multiple_of(their_cols + k * width, 128), width), :],
            preferred_element_type=F32,
        )
        acc[...] = total if k == 0 else acc[...] + total

    for step in range(pieces + 2):
        if step < pieces:
            stage_pack(step)
        if step == pieces:
            logits = remote(logit_out, logit_in, small_s.at[2], small_r.at[2], sib)
            logits.start()
            sends.append(logits)
        if 0 <= step - 1 < pieces:
            stage_forward(step - 1)
        if 0 <= step - 2:
            stage_up(step - 2)

    hid[...] = jax.nn.silu(acc[...]).astype(BF16)
    w_down_copy.wait()

    def stage_down(k):
        other = jnp.dot(
            hid[...], down_ref[:, pl.ds(pl.multiple_of(their_cols + k * width, 128), width)],
            preferred_element_type=F32,
        )
        part_out[k] = other.astype(BF16)
        copy = remote(part_out.at[k], part_in.at[k], part_s.at[k], part_r.at[k], sib)
        copy.start()
        sends.append(copy)
        own_part[k] = jnp.dot(
            hid[...], down_ref[:, pl.ds(pl.multiple_of(mine_cols + k * width, 128), width)],
            preferred_element_type=F32,
        ).astype(BF16)

    def stage_return(k):
        arrived(part_in.at[k], part_s.at[k], part_r.at[k])
        y = (own_part[k].astype(F32) + part_in[k].astype(F32)).astype(BF16)
        y = y.reshape(chips, padded, width)
        y_out[k] = y[1:]
        y_in[k, 0, 0:rows, :] = y[0, 0:rows]
        for d in order:
            copy = remote(
                y_out.at[k, d - 1, pl.ds(0, rows), :], y_in.at[k, d, pl.ds(0, rows), :],
                ret_s.at[k, d], ret_r.at[k, d], at_chip(d),
            )
            copy.start()
            sends.append(copy)

    for step in range(pieces + 1):
        if step < pieces:
            stage_down(step)
        if 0 <= step - 1:
            stage_return(step - 1)

    logits.wait_recv()
    picked = jnp.sum(onehot * (logit_out[...] + logit_in[...]), axis=0, keepdims=True)
    score = jax.nn.sigmoid(picked)
    score_ref[...] = jnp.transpose(jnp.broadcast_to(score, (128, count)))

    locals_ = []
    for k in range(pieces):
        for d in range(1, chips):
            arrived(y_in.at[k, d, pl.ds(0, rows), :], ret_s.at[k, d], ret_r.at[k, d])
        gathered = jnp.dot(
            place_t[...], y_in[k].reshape(chips * padded, width), preferred_element_type=F32
        )
        mixed = x_buf[k].astype(F32) + score_ref[:, 0:1] * gathered
        out_buf[k] = mixed.astype(BF16)
        cols = pl.ds(pl.multiple_of(mine_cols + k * width, 128), width)
        for m, out in enumerate((out_fwd, out_bwd)):
            theirs_at = pl.multiple_of((1 - core) * both + m * tokens, tokens)
            copy = remote(
                out_buf.at[k, pl.ds(theirs_at, tokens), :], out.at[:, cols],
                fin_s.at[k, m], fin_r.at[k, m], sib,
            )
            copy.start()
            sends.append(copy)
            mine_at = pl.multiple_of(core * both + m * tokens, tokens)
            local = pltpu.make_async_copy(
                out_buf.at[k, pl.ds(mine_at, tokens), :], out.at[:, cols], loc_s.at[k, m]
            )
            local.start()
            locals_.append(local)

    for local in locals_:
        local.wait()
    for k in range(pieces):
        other_cols = pl.ds(pl.multiple_of(their_cols + k * width, 128), width)
        for m, out in enumerate((out_fwd, out_bwd)):
            arrived(out.at[:, other_cols], fin_s.at[k, m], fin_r.at[k, m])
    for copy in sends:
        copy.wait_send()


def write_kernel(a_ref, b_ref, out_a, out_b, held, in_sem, out_sem):
    pairs = ((a_ref, out_a), (b_ref, out_b))
    loads = [pltpu.make_async_copy(src, held.at[i], in_sem.at[i]) for i, (src, _) in enumerate(pairs)]
    stores = [pltpu.make_async_copy(held.at[i], dst, out_sem.at[i]) for i, (_, dst) in enumerate(pairs)]
    for load in loads:
        load.start()
    for load, store in zip(loads, stores):
        load.wait()
        store.start()
    for store in stores:
        store.wait()


def on_device(sent_fwd, sent_bwd, router_w, w_up, w_down, routes_fwd, routes_bwd):
    tokens, model_width = sent_fwd.shape[1:]
    hidden = w_up.shape[2]
    sections = lax.axis_size("section")
    chips = lax.axis_size("expert") // 2
    per_expert = chips // EXPERTS
    rows = -(-4 * CAP // 8) * 8
    padded = -(-4 * CAP // 16) * 16
    pieces = PIECES
    width = model_width // 2 // pieces
    count = 4 * tokens
    dims = (chips, per_expert, sections, tokens, rows, padded, pieces, width)
    router = router_w[0].T
    total = chips * padded
    dma = pltpu.SemaphoreType.DMA
    any_space = pl.BlockSpec(memory_space=pl.ANY)
    vmem = pl.BlockSpec(memory_space=pltpu.VMEM)
    shape = jax.ShapeDtypeStruct((tokens, model_width), BF16)
    out_fwd, out_bwd = pl.pallas_call(
        functools.partial(layer_kernel, dims),
        out_shape=(shape, shape),
        in_specs=[vmem, vmem, any_space, any_space, vmem, any_space, any_space],
        out_specs=(any_space, any_space),
        scratch_shapes=[
            pltpu.VMEM((pieces, count, width), BF16),
            pltpu.VMEM((pieces, chips - 1, padded, width), BF16),
            pltpu.VMEM((pieces, chips, padded, width), BF16),
            pltpu.VMEM((pieces, chips, padded, width), BF16),
            pltpu.VMEM((total, hidden), F32),
            pltpu.VMEM((total, hidden), BF16),
            pltpu.VMEM((pieces, total, width), BF16),
            pltpu.VMEM((pieces, total, width), BF16),
            pltpu.VMEM((pieces, total, width), BF16),
            pltpu.VMEM((pieces, chips - 1, padded, width), BF16),
            pltpu.VMEM((pieces, chips, padded, width), BF16),
            pltpu.VMEM((pieces, count, width), BF16),
            pltpu.VMEM((model_width, hidden), BF16),
            pltpu.VMEM((hidden, model_width), BF16),
            pltpu.VMEM((total, count), BF16),
            pltpu.VMEM((count, total), BF16),
            pltpu.VMEM((2, 1, tokens), jnp.int32),
            pltpu.VMEM((EXPERTS, count), F32),
            pltpu.VMEM((EXPERTS, count), F32),
            pltpu.VMEM((count, 128), F32),
            dma((pieces, 2, 2)), dma((pieces, 2, 2)),
            dma((pieces, chips)), dma((pieces, chips)),
            dma((pieces, chips)), dma((pieces, chips)),
            dma((pieces,)), dma((pieces,)),
            dma((pieces, chips)), dma((pieces, chips)),
            dma((pieces, 2)), dma((pieces, 2)),
            dma((pieces, 2)), dma((2,)), dma((3,)), dma((3,)),
        ],
        compiler_params=pltpu.CompilerParams(collective_id=0, has_side_effects=True),
    )(
        routes_fwd.reshape(1, tokens), routes_bwd.reshape(1, tokens),
        sent_fwd[0], sent_bwd[0], router, w_up[0], w_down[0],
    )
    out_fwd, out_bwd = pl.pallas_call(
        write_kernel,
        out_shape=(shape, shape),
        in_specs=[any_space, any_space],
        out_specs=(any_space, any_space),
        scratch_shapes=[pltpu.VMEM((2, tokens, model_width), BF16), dma((2,)), dma((2,))],
        compiler_params=pltpu.CompilerParams(has_side_effects=True),
    )(out_fwd, out_bwd)
    return out_fwd[None], out_bwd[None]


def solution(mesh):
    return jax.shard_map(
        on_device,
        mesh=mesh,
        in_specs=(
            P("section", "expert", None),
            P("section", "expert", None),
            P("section", None, None),
            P("section", None, "expert"),
            P("section", "expert", None),
            P("section", "expert", None),
            P("section", "expert", None),
        ),
        out_specs=(P("section", "expert", None), P("section", "expert", None)),
        check_vma=False,
    )
```

```python
import functools

import jax
import jax.numpy as jnp
from jax import lax
from jax.experimental import pallas as pl
from jax.experimental.pallas import tpu as pltpu
from jax.sharding import PartitionSpec as P

EXPERTS = 4
CAP = 17
PIECES = 7
MESH = pl.DeviceIdType.MESH
F32 = jnp.float32
BF16 = jnp.bfloat16
NT = (((1,), (1,)), ((), ()))


def layer_kernel(
    dims,
    rf_ref, rb_ref, fwd_ref, bwd_ref, router_ref, up_hbm, down_hbm,
    out_fwd, out_bwd,
    x_buf, pack_buf, mine, theirs, acc, hid, part_out, part_in, own_part, y_out, y_in,
    out_buf, up_ref, down_ref, place, place_t, rt_sib, logit_out, logit_in, score_ref,
    relay_s, relay_r, disp_s, disp_r, pair_s, pair_r, part_s, part_r, ret_s, ret_r,
    fin_s, fin_r, loc_s, w_sem, small_s, small_r,
):
    chips, per_expert, sections, tokens, rows, padded, pieces, width = dims
    half = pieces * width
    both = 2 * tokens
    section = lax.axis_index("section")
    me = lax.axis_index("expert")
    core = lax.rem(me, 2)
    chip = me // 2
    sib = {"section": section, "expert": chip * 2 + 1 - core}
    after = lax.rem(section + 1, sections)
    before = lax.rem(section + sections - 1, sections)

    def partner(v):
        other, bit = chip, 1
        while bit <= v:
            if (v // bit) % 2:
                other = other + bit - 2 * bit * lax.rem(chip // bit, 2)
            bit *= 2
        return other

    def at_chip(v):
        return {"section": section, "expert": partner(v) * 2 + core}

    order = [v for v in range(chips // 2, chips)] + [v for v in range(1, chips // 2)]

    def remote(src, dst, send, recv, device):
        return pltpu.make_async_remote_copy(
            src_ref=src, dst_ref=dst, send_sem=send, recv_sem=recv,
            device_id=device, device_id_type=MESH,
        )

    def arrived(dst, send, recv):
        remote(dst, dst, send, recv, sib).wait_recv()

    w_up_copy = pltpu.make_async_copy(up_hbm, up_ref, w_sem.at[0])
    w_down_copy = pltpu.make_async_copy(down_hbm, down_ref, w_sem.at[1])

    tail = padded - 16
    zeros = jnp.zeros((pieces, chips, 16, width), BF16)
    mine[:, :, tail:padded, :] = zeros
    theirs[:, :, tail:padded, :] = zeros
    y_in[:, :, tail:padded, :] = zeros

    barrier = pltpu.get_barrier_semaphore()
    greet = [sib]
    for there in (after, before):
        for j in range(2):
            greet.append({"section": there, "expert": chip * 2 + j})
    for d in order:
        greet.append(at_chip(d))
    for device in greet:
        pl.semaphore_signal(barrier, inc=1, device_id=device, device_id_type=MESH)
    pl.semaphore_wait(barrier, len(greet))

    sends = []
    route_copies = []
    for m, ref in enumerate((rf_ref, rb_ref)):
        copy = remote(ref, rt_sib.at[m], small_s.at[m], small_r.at[m], sib)
        copy.start()
        sends.append(copy)
        route_copies.append(copy)
    for k in range(pieces):
        for m, (source, there) in enumerate(((fwd_ref, after), (bwd_ref, before))):
            for j in range(2):
                copy = remote(
                    source.at[:, pl.ds(j * half + k * width, width)],
                    x_buf.at[k, pl.ds(pl.multiple_of(core * both + m * tokens, tokens), tokens), :],
                    relay_s.at[k, j, m], relay_r.at[k, core, m],
                    {"section": there, "expert": chip * 2 + j},
                )
                copy.start()
                sends.append(copy)
    w_up_copy.start()
    w_down_copy.start()

    for copy in route_copies:
        copy.wait_recv()
    own = (rf_ref[...], rb_ref[...])
    sibs = (rt_sib[0], rt_sib[1])
    first = core == 0
    chosen = jnp.concatenate(
        [jnp.where(first, a, b) for a, b in zip(own, sibs)]
        + [jnp.where(first, b, a) for a, b in zip(own, sibs)],
        axis=1,
    )
    count = 2 * both
    named = lax.broadcasted_iota(jnp.int32, (EXPERTS, count), 0) == chosen
    onehot = jnp.where(named, 1.0, 0.0).astype(F32)
    earlier = lax.broadcasted_iota(jnp.int32, (count, count), 0) <= lax.broadcasted_iota(
        jnp.int32, (count, count), 1
    )
    tri = jnp.where(earlier, 1.0, 0.0).astype(BF16)
    counted = jnp.dot(onehot.astype(BF16), tri, preferred_element_type=F32)
    position = jnp.sum(onehot * (counted - 1.0), axis=0, keepdims=True)
    slots = lax.broadcasted_iota(jnp.int32, (padded, count), 0).astype(F32)
    for d in range(chips):
        expert = partner(d) // per_expert
        here = jnp.where(chosen == expert, position, -1.0)
        place[d * padded:(d + 1) * padded, :] = jnp.where(slots == here, 1.0, 0.0).astype(BF16)
    eye = lax.broadcasted_iota(jnp.int32, (count, count), 0) == lax.broadcasted_iota(
        jnp.int32, (count, count), 1
    )
    eye = jnp.where(eye, 1.0, 0.0).astype(BF16)
    place_t[...] = lax.dot_general(eye, place[...], NT, preferred_element_type=F32).astype(BF16)

    mine_cols = core * half
    their_cols = (1 - core) * half

    def pair(k, d):
        copy = remote(mine.at[k, d], theirs.at[k, d], pair_s.at[k, d], pair_r.at[k, d], sib)
        copy.start()
        sends.append(copy)

    def stage_pack(k):
        for j in range(2):
            for m in range(2):
                arrived(
                    x_buf.at[k, pl.ds(j * both + m * tokens, tokens), :],
                    relay_s.at[k, j, m], relay_r.at[k, j, m],
                )
        packed = jnp.dot(place[...], x_buf[k], preferred_element_type=F32).astype(BF16)
        packed = packed.reshape(chips, padded, width)
        pack_buf[k] = packed[1:]
        mine[k, 0] = packed[0]
        for d in order:
            copy = remote(
                pack_buf.at[k, d - 1, pl.ds(0, rows), :], mine.at[k, d, pl.ds(0, rows), :],
                disp_s.at[k, d], disp_r.at[k, d], at_chip(d),
            )
            copy.start()
            sends.append(copy)
        pair(k, 0)

    def stage_forward(k):
        for d in order:
            arrived(mine.at[k, d, pl.ds(0, rows), :], disp_s.at[k, d], disp_r.at[k, d])
            pair(k, d)

    def stage_up(k):
        if k == 0:
            w_up_copy.wait()
        total = jnp.dot(
            mine[k].reshape(chips * padded, width),
            up_ref[pl.ds(pl.multiple_of(mine_cols + k * width, 128), width), :],
            preferred_element_type=F32,
        )
        for d in range(chips):
            arrived(theirs.at[k, d], pair_s.at[k, d], pair_r.at[k, d])
        total += jnp.dot(
            theirs[k].reshape(chips * padded, width),
            up_ref[pl.ds(pl.multiple_of(their_cols + k * width, 128), width), :],
            preferred_element_type=F32,
        )
        acc[...] = total if k == 0 else acc[...] + total

    for step in range(pieces + 2):
        if step < pieces:
            stage_pack(step)
        if step >= pieces:
            stage_up(step - 2)
        if 0 <= step - 1 < pieces:
            stage_forward(step - 1)
        if 0 <= step - 2 < pieces - 2:
            stage_up(step - 2)

    hid[...] = jax.nn.silu(acc[...]).astype(BF16)
    w_down_copy.wait()

    def stage_down(k):
        other = jnp.dot(
            hid[...], down_ref[:, pl.ds(pl.multiple_of(their_cols + k * width, 128), width)],
            preferred_element_type=F32,
        )
        part_out[k] = other.astype(BF16)
        copy = remote(part_out.at[k], part_in.at[k], part_s.at[k], part_r.at[k], sib)
        copy.start()
        sends.append(copy)
        own_part[k] = jnp.dot(
            hid[...], down_ref[:, pl.ds(pl.multiple_of(mine_cols + k * width, 128), width)],
            preferred_element_type=F32,
        ).astype(BF16)

    def stage_return(k):
        arrived(part_in.at[k], part_s.at[k], part_r.at[k])
        y = (own_part[k].astype(F32) + part_in[k].astype(F32)).astype(BF16)
        y = y.reshape(chips, padded, width)
        y_out[k] = y[1:]
        y_in[k, 0, 0:rows, :] = y[0, 0:rows]
        for d in order:
            copy = remote(
                y_out.at[k, d - 1, pl.ds(0, rows), :], y_in.at[k, d, pl.ds(0, rows), :],
                ret_s.at[k, d], ret_r.at[k, d], at_chip(d),
            )
            copy.start()
            sends.append(copy)

    for step in range(pieces + 1):
        if step < pieces:
            stage_down(step)
        if 0 <= step - 1:
            stage_return(step - 1)

    for k in range(pieces):
        cols = pl.ds(pl.multiple_of(mine_cols + k * width, 128), width)
        term = lax.dot_general(
            router_ref[:, cols], x_buf[k].astype(F32), NT,
            precision=lax.Precision.HIGHEST, preferred_element_type=F32,
        )
        logit_out[...] = term if k == 0 else logit_out[...] + term
    logits = remote(logit_out, logit_in, small_s.at[2], small_r.at[2], sib)
    logits.start()
    sends.append(logits)
    logits.wait_recv()
    picked = jnp.sum(onehot * (logit_out[...] + logit_in[...]), axis=0, keepdims=True)
    score = jax.nn.sigmoid(picked)
    score_ref[...] = jnp.transpose(jnp.broadcast_to(score, (128, count)))

    locals_ = []
    for k in range(pieces):
        for d in range(1, chips):
            arrived(y_in.at[k, d, pl.ds(0, rows), :], ret_s.at[k, d], ret_r.at[k, d])
        gathered = jnp.dot(
            place_t[...], y_in[k].reshape(chips * padded, width), preferred_element_type=F32
        )
        mixed = x_buf[k].astype(F32) + score_ref[:, 0:1] * gathered
        out_buf[k] = mixed.astype(BF16)
        cols = pl.ds(pl.multiple_of(mine_cols + k * width, 128), width)
        for m, out in enumerate((out_fwd, out_bwd)):
            theirs_at = pl.multiple_of((1 - core) * both + m * tokens, tokens)
            copy = remote(
                out_buf.at[k, pl.ds(theirs_at, tokens), :], out.at[:, cols],
                fin_s.at[k, m], fin_r.at[k, m], sib,
            )
            copy.start()
            sends.append(copy)
            mine_at = pl.multiple_of(core * both + m * tokens, tokens)
            local = pltpu.make_async_copy(
                out_buf.at[k, pl.ds(mine_at, tokens), :], out.at[:, cols], loc_s.at[k, m]
            )
            local.start()
            locals_.append(local)

    for local in locals_:
        local.wait()
    for k in range(pieces):
        other_cols = pl.ds(pl.multiple_of(their_cols + k * width, 128), width)
        for m, out in enumerate((out_fwd, out_bwd)):
            arrived(out.at[:, other_cols], fin_s.at[k, m], fin_r.at[k, m])
    for copy in sends:
        copy.wait_send()


def write_kernel(a_ref, b_ref, out_a, out_b, held, in_sem, out_sem):
    pairs = ((a_ref, out_a), (b_ref, out_b))
    loads = [pltpu.make_async_copy(src, held.at[i], in_sem.at[i]) for i, (src, _) in enumerate(pairs)]
    stores = [pltpu.make_async_copy(held.at[i], dst, out_sem.at[i]) for i, (_, dst) in enumerate(pairs)]
    for load in loads:
        load.start()
    for load, store in zip(loads, stores):
        load.wait()
        store.start()
    for store in stores:
        store.wait()


def on_device(sent_fwd, sent_bwd, router_w, w_up, w_down, routes_fwd, routes_bwd):
    tokens, model_width = sent_fwd.shape[1:]
    hidden = w_up.shape[2]
    sections = lax.axis_size("section")
    chips = lax.axis_size("expert") // 2
    per_expert = chips // EXPERTS
    rows = -(-4 * CAP // 8) * 8
    padded = -(-4 * CAP // 16) * 16
    pieces = PIECES
    width = model_width // 2 // pieces
    count = 4 * tokens
    dims = (chips, per_expert, sections, tokens, rows, padded, pieces, width)
    router = router_w[0].T
    total = chips * padded
    dma = pltpu.SemaphoreType.DMA
    any_space = pl.BlockSpec(memory_space=pl.ANY)
    vmem = pl.BlockSpec(memory_space=pltpu.VMEM)
    shape = jax.ShapeDtypeStruct((tokens, model_width), BF16)
    out_fwd, out_bwd = pl.pallas_call(
        functools.partial(layer_kernel, dims),
        out_shape=(shape, shape),
        in_specs=[vmem, vmem, any_space, any_space, vmem, any_space, any_space],
        out_specs=(any_space, any_space),
        scratch_shapes=[
            pltpu.VMEM((pieces, count, width), BF16),
            pltpu.VMEM((pieces, chips - 1, padded, width), BF16),
            pltpu.VMEM((pieces, chips, padded, width), BF16),
            pltpu.VMEM((pieces, chips, padded, width), BF16),
            pltpu.VMEM((total, hidden), F32),
            pltpu.VMEM((total, hidden), BF16),
            pltpu.VMEM((pieces, total, width), BF16),
            pltpu.VMEM((pieces, total, width), BF16),
            pltpu.VMEM((pieces, total, width), BF16),
            pltpu.VMEM((pieces, chips - 1, padded, width), BF16),
            pltpu.VMEM((pieces, chips, padded, width), BF16),
            pltpu.VMEM((pieces, count, width), BF16),
            pltpu.VMEM((model_width, hidden), BF16),
            pltpu.VMEM((hidden, model_width), BF16),
            pltpu.VMEM((total, count), BF16),
            pltpu.VMEM((count, total), BF16),
            pltpu.VMEM((2, 1, tokens), jnp.int32),
            pltpu.VMEM((EXPERTS, count), F32),
            pltpu.VMEM((EXPERTS, count), F32),
            pltpu.VMEM((count, 128), F32),
            dma((pieces, 2, 2)), dma((pieces, 2, 2)),
            dma((pieces, chips)), dma((pieces, chips)),
            dma((pieces, chips)), dma((pieces, chips)),
            dma((pieces,)), dma((pieces,)),
            dma((pieces, chips)), dma((pieces, chips)),
            dma((pieces, 2)), dma((pieces, 2)),
            dma((pieces, 2)), dma((2,)), dma((3,)), dma((3,)),
        ],
        compiler_params=pltpu.CompilerParams(collective_id=0, has_side_effects=True),
    )(
        routes_fwd.reshape(1, tokens), routes_bwd.reshape(1, tokens),
        sent_fwd[0], sent_bwd[0], router, w_up[0], w_down[0],
    )
    out_fwd, out_bwd = pl.pallas_call(
        write_kernel,
        out_shape=(shape, shape),
        in_specs=[any_space, any_space],
        out_specs=(any_space, any_space),
        scratch_shapes=[pltpu.VMEM((2, tokens, model_width), BF16), dma((2,)), dma((2,))],
        compiler_params=pltpu.CompilerParams(has_side_effects=True),
    )(out_fwd, out_bwd)
    return out_fwd[None], out_bwd[None]


def solution(mesh):
    return jax.shard_map(
        on_device,
        mesh=mesh,
        in_specs=(
            P("section", "expert", None),
            P("section", "expert", None),
            P("section", None, None),
            P("section", None, "expert"),
            P("section", "expert", None),
            P("section", "expert", None),
            P("section", "expert", None),
        ),
        out_specs=(P("section", "expert", None), P("section", "expert", None)),
        check_vma=False,
    )
```

```python
import functools

import jax
import jax.numpy as jnp
from jax import lax
from jax.experimental import pallas as pl
from jax.experimental.pallas import tpu as pltpu
from jax.sharding import PartitionSpec as P

EXPERTS = 4
CAP = 17
PIECES = 7
MESH = pl.DeviceIdType.MESH
F32 = jnp.float32
BF16 = jnp.bfloat16
NT = (((1,), (1,)), ((), ()))


def layer_kernel(
    dims,
    rf_ref, rb_ref, fwd_hbm, bwd_hbm, router_ref, up_hbm, down_hbm,
    out_fwd, out_bwd,
    fwd_ref, bwd_ref, in_s, x_buf, pack_buf, mine, theirs, acc, hid, part_out, part_in, own_part, y_out, y_in,
    out_buf, up_ref, down_ref, place, place_t, rt_sib, logit_out, logit_in, score_ref,
    relay_s, relay_r, disp_s, disp_r, pair_s, pair_r, part_s, part_r, ret_s, ret_r,
    fin_s, fin_r, loc_s, w_sem, small_s, small_r,
):
    chips, per_expert, sections, tokens, rows, padded, pieces, width = dims
    half = pieces * width
    both = 2 * tokens
    section = lax.axis_index("section")
    me = lax.axis_index("expert")
    core = lax.rem(me, 2)
    chip = me // 2
    sib = {"section": section, "expert": chip * 2 + 1 - core}
    after = lax.rem(section + 1, sections)
    before = lax.rem(section + sections - 1, sections)

    def partner(v):
        other, bit = chip, 1
        while bit <= v:
            if (v // bit) % 2:
                other = other + bit - 2 * bit * lax.rem(chip // bit, 2)
            bit *= 2
        return other

    def at_chip(v):
        return {"section": section, "expert": partner(v) * 2 + core}

    order = [v for v in range(chips // 2, chips)] + [v for v in range(1, chips // 2)]

    def remote(src, dst, send, recv, device):
        return pltpu.make_async_remote_copy(
            src_ref=src, dst_ref=dst, send_sem=send, recv_sem=recv,
            device_id=device, device_id_type=MESH,
        )

    def arrived(dst, send, recv):
        remote(dst, dst, send, recv, sib).wait_recv()

    w_up_copy = pltpu.make_async_copy(up_hbm, up_ref, w_sem.at[0])
    w_down_copy = pltpu.make_async_copy(down_hbm, down_ref, w_sem.at[1])

    loads = [
        pltpu.make_async_copy(fwd_hbm, fwd_ref, in_s.at[0]),
        pltpu.make_async_copy(bwd_hbm, bwd_ref, in_s.at[1]),
    ]
    for load in loads:
        load.start()

    tail = padded - 16
    zeros = jnp.zeros((pieces, chips, 16, width), BF16)
    mine[:, :, tail:padded, :] = zeros
    theirs[:, :, tail:padded, :] = zeros
    y_in[:, :, tail:padded, :] = zeros

    barrier = pltpu.get_barrier_semaphore()
    greet = [sib]
    for there in (after, before):
        for j in range(2):
            greet.append({"section": there, "expert": chip * 2 + j})
    for d in order:
        greet.append(at_chip(d))
    for device in greet:
        pl.semaphore_signal(barrier, inc=1, device_id=device, device_id_type=MESH)
    pl.semaphore_wait(barrier, len(greet))
    for load in loads:
        load.wait()

    sends = []
    route_copies = []
    for m, ref in enumerate((rf_ref, rb_ref)):
        copy = remote(ref, rt_sib.at[m], small_s.at[m], small_r.at[m], sib)
        copy.start()
        sends.append(copy)
        route_copies.append(copy)
    for k in range(pieces):
        for m, (source, there) in enumerate(((fwd_ref, after), (bwd_ref, before))):
            for j in range(2):
                copy = remote(
                    source.at[:, pl.ds(j * half + k * width, width)],
                    x_buf.at[k, pl.ds(pl.multiple_of(core * both + m * tokens, tokens), tokens), :],
                    relay_s.at[k, j, m], relay_r.at[k, core, m],
                    {"section": there, "expert": chip * 2 + j},
                )
                copy.start()
                sends.append(copy)
    w_up_copy.start()
    w_down_copy.start()

    for copy in route_copies:
        copy.wait_recv()
    own = (rf_ref[...], rb_ref[...])
    sibs = (rt_sib[0], rt_sib[1])
    first = core == 0
    chosen = jnp.concatenate(
        [jnp.where(first, a, b) for a, b in zip(own, sibs)]
        + [jnp.where(first, b, a) for a, b in zip(own, sibs)],
        axis=1,
    )
    count = 2 * both
    named = lax.broadcasted_iota(jnp.int32, (EXPERTS, count), 0) == chosen
    onehot = jnp.where(named, 1.0, 0.0).astype(F32)
    earlier = lax.broadcasted_iota(jnp.int32, (count, count), 0) <= lax.broadcasted_iota(
        jnp.int32, (count, count), 1
    )
    tri = jnp.where(earlier, 1.0, 0.0).astype(BF16)
    counted = jnp.dot(onehot.astype(BF16), tri, preferred_element_type=F32)
    position = jnp.sum(onehot * (counted - 1.0), axis=0, keepdims=True)
    slots = lax.broadcasted_iota(jnp.int32, (padded, count), 0).astype(F32)
    for d in range(chips):
        expert = partner(d) // per_expert
        here = jnp.where(chosen == expert, position, -1.0)
        place[d * padded:(d + 1) * padded, :] = jnp.where(slots == here, 1.0, 0.0).astype(BF16)
    eye = lax.broadcasted_iota(jnp.int32, (count, count), 0) == lax.broadcasted_iota(
        jnp.int32, (count, count), 1
    )
    eye = jnp.where(eye, 1.0, 0.0).astype(BF16)
    place_t[...] = lax.dot_general(eye, place[...], NT, preferred_element_type=F32).astype(BF16)

    mine_cols = core * half
    their_cols = (1 - core) * half

    def pair(k, d):
        copy = remote(mine.at[k, d], theirs.at[k, d], pair_s.at[k, d], pair_r.at[k, d], sib)
        copy.start()
        sends.append(copy)

    def stage_pack(k):
        for j in range(2):
            for m in range(2):
                arrived(
                    x_buf.at[k, pl.ds(j * both + m * tokens, tokens), :],
                    relay_s.at[k, j, m], relay_r.at[k, j, m],
                )
        packed = jnp.dot(place[...], x_buf[k], preferred_element_type=F32).astype(BF16)
        packed = packed.reshape(chips, padded, width)
        pack_buf[k] = packed[1:]
        mine[k, 0] = packed[0]
        for d in order:
            copy = remote(
                pack_buf.at[k, d - 1, pl.ds(0, rows), :], mine.at[k, d, pl.ds(0, rows), :],
                disp_s.at[k, d], disp_r.at[k, d], at_chip(d),
            )
            copy.start()
            sends.append(copy)
        pair(k, 0)

    def stage_forward(k):
        for d in order:
            arrived(mine.at[k, d, pl.ds(0, rows), :], disp_s.at[k, d], disp_r.at[k, d])
            pair(k, d)

    def stage_up(k):
        if k == 0:
            w_up_copy.wait()
        total = jnp.dot(
            mine[k].reshape(chips * padded, width),
            up_ref[pl.ds(pl.multiple_of(mine_cols + k * width, 128), width), :],
            preferred_element_type=F32,
        )
        for d in range(chips):
            arrived(theirs.at[k, d], pair_s.at[k, d], pair_r.at[k, d])
        total += jnp.dot(
            theirs[k].reshape(chips * padded, width),
            up_ref[pl.ds(pl.multiple_of(their_cols + k * width, 128), width), :],
            preferred_element_type=F32,
        )
        acc[...] = total if k == 0 else acc[...] + total

    for step in range(pieces + 2):
        if step < pieces:
            stage_pack(step)
        if step >= pieces:
            stage_up(step - 2)
        if 0 <= step - 1 < pieces:
            stage_forward(step - 1)
        if 0 <= step - 2 < pieces - 2:
            stage_up(step - 2)

    hid[...] = jax.nn.silu(acc[...]).astype(BF16)
    w_down_copy.wait()

    def stage_down(k):
        other = jnp.dot(
            hid[...], down_ref[:, pl.ds(pl.multiple_of(their_cols + k * width, 128), width)],
            preferred_element_type=F32,
        )
        part_out[k] = other.astype(BF16)
        copy = remote(part_out.at[k], part_in.at[k], part_s.at[k], part_r.at[k], sib)
        copy.start()
        sends.append(copy)
        own_part[k] = jnp.dot(
            hid[...], down_ref[:, pl.ds(pl.multiple_of(mine_cols + k * width, 128), width)],
            preferred_element_type=F32,
        ).astype(BF16)

    def stage_return(k):
        arrived(part_in.at[k], part_s.at[k], part_r.at[k])
        y = (own_part[k].astype(F32) + part_in[k].astype(F32)).astype(BF16)
        y = y.reshape(chips, padded, width)
        y_out[k] = y[1:]
        y_in[k, 0, 0:rows, :] = y[0, 0:rows]
        for d in order:
            copy = remote(
                y_out.at[k, d - 1, pl.ds(0, rows), :], y_in.at[k, d, pl.ds(0, rows), :],
                ret_s.at[k, d], ret_r.at[k, d], at_chip(d),
            )
            copy.start()
            sends.append(copy)

    for step in range(pieces + 1):
        if step < pieces:
            stage_down(step)
        if 0 <= step - 1:
            stage_return(step - 1)

    for k in range(pieces):
        cols = pl.ds(pl.multiple_of(mine_cols + k * width, 128), width)
        term = lax.dot_general(
            router_ref[:, cols], x_buf[k].astype(F32), NT,
            precision=lax.Precision.HIGHEST, preferred_element_type=F32,
        )
        logit_out[...] = term if k == 0 else logit_out[...] + term
    logits = remote(logit_out, logit_in, small_s.at[2], small_r.at[2], sib)
    logits.start()
    sends.append(logits)
    logits.wait_recv()
    picked = jnp.sum(onehot * (logit_out[...] + logit_in[...]), axis=0, keepdims=True)
    score = jax.nn.sigmoid(picked)
    score_ref[...] = jnp.transpose(jnp.broadcast_to(score, (128, count)))

    locals_ = []
    for k in range(pieces):
        for d in range(1, chips):
            arrived(y_in.at[k, d, pl.ds(0, rows), :], ret_s.at[k, d], ret_r.at[k, d])
        gathered = jnp.dot(
            place_t[...], y_in[k].reshape(chips * padded, width), preferred_element_type=F32
        )
        mixed = x_buf[k].astype(F32) + score_ref[:, 0:1] * gathered
        out_buf[k] = mixed.astype(BF16)
        cols = pl.ds(pl.multiple_of(mine_cols + k * width, 128), width)
        for m, out in enumerate((out_fwd, out_bwd)):
            theirs_at = pl.multiple_of((1 - core) * both + m * tokens, tokens)
            copy = remote(
                out_buf.at[k, pl.ds(theirs_at, tokens), :], out.at[:, cols],
                fin_s.at[k, m], fin_r.at[k, m], sib,
            )
            copy.start()
            sends.append(copy)
            mine_at = pl.multiple_of(core * both + m * tokens, tokens)
            local = pltpu.make_async_copy(
                out_buf.at[k, pl.ds(mine_at, tokens), :], out.at[:, cols], loc_s.at[k, m]
            )
            local.start()
            locals_.append(local)

    for local in locals_:
        local.wait()
    for k in range(pieces):
        other_cols = pl.ds(pl.multiple_of(their_cols + k * width, 128), width)
        for m, out in enumerate((out_fwd, out_bwd)):
            arrived(out.at[:, other_cols], fin_s.at[k, m], fin_r.at[k, m])
    for copy in sends:
        copy.wait_send()


def write_kernel(a_ref, b_ref, out_a, out_b, held, in_sem, out_sem):
    pairs = ((a_ref, out_a), (b_ref, out_b))
    loads = [pltpu.make_async_copy(src, held.at[i], in_sem.at[i]) for i, (src, _) in enumerate(pairs)]
    stores = [pltpu.make_async_copy(held.at[i], dst, out_sem.at[i]) for i, (_, dst) in enumerate(pairs)]
    for load in loads:
        load.start()
    for load, store in zip(loads, stores):
        load.wait()
        store.start()
    for store in stores:
        store.wait()


def on_device(sent_fwd, sent_bwd, router_w, w_up, w_down, routes_fwd, routes_bwd):
    tokens, model_width = sent_fwd.shape[1:]
    hidden = w_up.shape[2]
    sections = lax.axis_size("section")
    chips = lax.axis_size("expert") // 2
    per_expert = chips // EXPERTS
    rows = -(-4 * CAP // 8) * 8
    padded = -(-4 * CAP // 16) * 16
    pieces = PIECES
    width = model_width // 2 // pieces
    count = 4 * tokens
    dims = (chips, per_expert, sections, tokens, rows, padded, pieces, width)
    router = router_w[0].T
    total = chips * padded
    dma = pltpu.SemaphoreType.DMA
    any_space = pl.BlockSpec(memory_space=pl.ANY)
    vmem = pl.BlockSpec(memory_space=pltpu.VMEM)
    shape = jax.ShapeDtypeStruct((tokens, model_width), BF16)
    out_fwd, out_bwd = pl.pallas_call(
        functools.partial(layer_kernel, dims),
        out_shape=(shape, shape),
        in_specs=[vmem, vmem, any_space, any_space, vmem, any_space, any_space],
        out_specs=(any_space, any_space),
        scratch_shapes=[
            pltpu.VMEM((tokens, model_width), BF16),
            pltpu.VMEM((tokens, model_width), BF16),
            dma((2,)),
            pltpu.VMEM((pieces, count, width), BF16),
            pltpu.VMEM((pieces, chips - 1, padded, width), BF16),
            pltpu.VMEM((pieces, chips, padded, width), BF16),
            pltpu.VMEM((pieces, chips, padded, width), BF16),
            pltpu.VMEM((total, hidden), F32),
            pltpu.VMEM((total, hidden), BF16),
            pltpu.VMEM((pieces, total, width), BF16),
            pltpu.VMEM((pieces, total, width), BF16),
            pltpu.VMEM((pieces, total, width), BF16),
            pltpu.VMEM((pieces, chips - 1, padded, width), BF16),
            pltpu.VMEM((pieces, chips, padded, width), BF16),
            pltpu.VMEM((pieces, count, width), BF16),
            pltpu.VMEM((model_width, hidden), BF16),
            pltpu.VMEM((hidden, model_width), BF16),
            pltpu.VMEM((total, count), BF16),
            pltpu.VMEM((count, total), BF16),
            pltpu.VMEM((2, 1, tokens), jnp.int32),
            pltpu.VMEM((EXPERTS, count), F32),
            pltpu.VMEM((EXPERTS, count), F32),
            pltpu.VMEM((count, 128), F32),
            dma((pieces, 2, 2)), dma((pieces, 2, 2)),
            dma((pieces, chips)), dma((pieces, chips)),
            dma((pieces, chips)), dma((pieces, chips)),
            dma((pieces,)), dma((pieces,)),
            dma((pieces, chips)), dma((pieces, chips)),
            dma((pieces, 2)), dma((pieces, 2)),
            dma((pieces, 2)), dma((2,)), dma((3,)), dma((3,)),
        ],
        compiler_params=pltpu.CompilerParams(collective_id=0, has_side_effects=True),
    )(
        routes_fwd.reshape(1, tokens), routes_bwd.reshape(1, tokens),
        sent_fwd[0], sent_bwd[0], router, w_up[0], w_down[0],
    )
    out_fwd, out_bwd = pl.pallas_call(
        write_kernel,
        out_shape=(shape, shape),
        in_specs=[any_space, any_space],
        out_specs=(any_space, any_space),
        scratch_shapes=[pltpu.VMEM((2, tokens, model_width), BF16), dma((2,)), dma((2,))],
        compiler_params=pltpu.CompilerParams(has_side_effects=True),
    )(out_fwd, out_bwd)
    return out_fwd[None], out_bwd[None]


def solution(mesh):
    return jax.shard_map(
        on_device,
        mesh=mesh,
        in_specs=(
            P("section", "expert", None),
            P("section", "expert", None),
            P("section", None, None),
            P("section", None, "expert"),
            P("section", "expert", None),
            P("section", "expert", None),
            P("section", "expert", None),
        ),
        out_specs=(P("section", "expert", None), P("section", "expert", None)),
        check_vma=False,
    )
```
